32 devices in a mesh: dp: 4 (over y, x), tensor: 8 (over z, core).
Axes of the slice: x: 2, y: 2, z: 4, core: 2. Of those that a mesh axis runs over, the one named last changes fastest.
Arguments:
- tokens: bfloat16 [8, 256, 8192], P('dp'), may hold values from -6 to 6
- segments: int32 [8, 256], P('dp'), may hold values from 0 to 3, never falling along the last dimension, each value on 1 to 128 neighbouring positions
- norm_gain: float32 [8192], replicated, may hold values from 0.25 to 3.5
- q_weight: bfloat16 [8192, 4096], P('dp', 'tensor'), may hold values from -1.3479223 to 1.3479223
- kv_weight: bfloat16 [2, 8192, 512], P(None, 'dp'), may hold values from -0.055242717 to 0.055242717
- o_weight: bfloat16 [4096, 8192], P('tensor', 'dp'), may hold values from -0.09375 to 0.09375
- basis_query: bfloat16 [8, 8192, 4096], P(None, 'dp', 'tensor'), may hold values from -11 to 11
- basis_output: bfloat16 [8, 4096, 8192], P(None, 'tensor', 'dp'), may hold values from -11 to 11
Outputs:
- next_query: bfloat16 [8192, 4096], P('dp', 'tensor')
- next_output: bfloat16 [4096, 8192], P('tensor', 'dp')
- coefficients: float32 [9], replicated
The draws below stay inside these ranges and needn't reach their ends.
Inputs may be any that keep to these rules, and one draw needn't show every extreme that they name: `segments`: segment numbers never fall along a sequence.
All inputs are finite; a program needn't handle non-finite values.
Results may differ from the reference program's by a relative error of at most 0.018.
Values may be sent and summed in bfloat16 or wider, within the bound.
No kernel may reach another device: no remote copies, remote signals or barrier semaphores. Data moves between devices by JAX's collectives and lax.ppermute only.
A program may use at most 192 MiB of HBM per device.

```python
import math
import jax
import jax.numpy as jnp
import numpy as np
from jax import lax

D = 8192
HD = 128
QH = 32
KVH = 4
LEN = 256
K = 8
SEQUENCES = 8
N_DP = 4
N_TENSOR = 8


def feature_ramp(low, high):
    return low + (high - low) * jnp.arange(D, dtype=jnp.float32) / (D - 1.0)


def shared_projections(key):
    base_key = jax.random.fold_in(key, 4242)
    kv_width = KVH * HD
    key_part = jnp.clip(jax.random.normal(jax.random.fold_in(base_key, 1), (D, kv_width), jnp.float32), -5.0, 5.0) / math.sqrt(D)
    value_part = jnp.clip(jax.random.normal(jax.random.fold_in(base_key, 2), (D, kv_width), jnp.float32), -5.0, 5.0) / math.sqrt(D)
    query_noise = jnp.clip(jax.random.normal(jax.random.fold_in(base_key, 3), (D, QH * HD), jnp.float32), -5.0, 5.0) / math.sqrt(D)
    query_part = query_noise
    return (query_part, jnp.stack([key_part, value_part]))


def basis_vectors(key, out_shape):
    common = jnp.clip(jax.random.normal(jax.random.fold_in(key, 2), out_shape[1:], jnp.float32), -4.0, 4.0)
    independent = jnp.clip(jax.random.normal(jax.random.fold_in(key, 1), out_shape, jnp.float32), -4.0, 4.0)
    return ((independent + 0.6 * common[None]) / math.sqrt(1.36), feature_ramp(0.4, 2.0))


def draw_norm_gain(key, part):
    jitter = jax.random.uniform(jax.random.fold_in(key, 77), (D,), jnp.float32, 0.85, 1.15)
    return jitter * feature_ramp(0.5, 2.0)


def draw_q_weight(key, part):
    return shared_projections(key)[0].astype(jnp.bfloat16)


def draw_kv_weight(key, part):
    return shared_projections(key)[1].astype(jnp.bfloat16)


def draw_basis_query(key, part):
    values, ramp = basis_vectors(jax.random.fold_in(key, 11), (K, D, QH * HD))
    return (values * ramp[None, :, None]).astype(jnp.bfloat16)


def draw_basis_output(key, part):
    values, ramp = basis_vectors(jax.random.fold_in(key, 13), (K, QH * HD, D))
    return (values * ramp[None, None, :]).astype(jnp.bfloat16)


def steps_of(rng, dims, cuts, least, top_value):
    def one(axis_at, parts):
        steps = jax.random.uniform(jax.random.fold_in(jax.random.fold_in(rng, 6), axis_at), (parts,), jnp.float32, least / len(cuts), top_value / len(cuts))
        return jnp.repeat(jnp.exp(steps), dims[axis_at] // parts).reshape((-1,) + (1,) * (len(dims) - axis_at - 1))

    level = one(*cuts[0])
    for cut in cuts[1:]:
        level = level * one(*cut)
    return level


def profile(count, total, reach, lean):
    portions = [(1 << 20) // math.isqrt(standing ** lean) + 1 for standing in range(2, count + 1)]
    rest, holding = total - reach - (count - 1), [1] * (count - 1)
    while rest > 0:
        candidates = [i for i in range(count - 1) if holding[i] < reach]
        whole, remaining = sum([portions[i] for i in candidates]), rest
        for i in candidates:
            more = min(reach - holding[i], max(1, remaining * portions[i] // whole), rest)
            holding[i] = holding[i] + more
            rest = rest - more
    return np.array([reach] + holding)


def uneven(stream_key, count, total, reach, skew):
    if count == 2:
        one = jax.random.randint(stream_key, (), max(1, total - reach), min(reach, total - 1) + 1)
        return jnp.stack([one, total - one])
    tallies = jnp.asarray(profile(count, total, reach, skew), jnp.int32)
    pairs = (count - 1) // 2
    donor, receiver = tallies[1:1 + 2 * pairs:2], tallies[2:2 + 2 * pairs:2]
    slack = jnp.minimum(donor - 1, reach - receiver)
    passed = jax.random.randint(jax.random.fold_in(stream_key, 1), (pairs,), 0, 1 << 20) % (slack + 1)
    tallies = tallies.at[1:1 + 2 * pairs:2].set(donor - passed).at[2:2 + 2 * pairs:2].set(receiver + passed)
    return tallies[jax.random.permutation(jax.random.fold_in(stream_key, 2), count)]


def gaussian(own_key, shape, scale, limit, pieces=(), held_as=jnp.bfloat16):
    values = jax.random.normal(own_key, shape, jnp.float32) * scale
    if len(pieces) > 0:
        values = steps_of(own_key, shape, pieces, -0.22, 0.18) * values
    return jnp.clip(values, min=-limit, max=limit).astype(held_as)


def setup_inputs(seed: int = 0) -> dict:
    arg_keys = jax.random.split(jax.random.key(seed), 9)
    tokens = gaussian(arg_keys[0], (SEQUENCES, LEN, D), 1.0, 6.0, ((0, 4),))
    segments = jax.vmap(lambda own: jnp.searchsorted(jnp.cumsum(uneven(own, 4, LEN, LEN // 2, 0)), jnp.arange(LEN), side="right"))(jax.random.split(arg_keys[1], SEQUENCES)).reshape((SEQUENCES, LEN)).astype(jnp.int32)
    norm_gain = draw_norm_gain(jax.random.fold_in(arg_keys[8], 71), 0)
    q_weight = draw_q_weight(jax.random.fold_in(arg_keys[8], 71), 0)
    kv_weight = draw_kv_weight(jax.random.fold_in(arg_keys[8], 71), 0)
    o_weight = gaussian(arg_keys[5], (QH * HD, D), (QH * HD) ** -0.5, 0.09375, ((0, 8), (1, 4)))
    basis_query = draw_basis_query(jax.random.fold_in(arg_keys[8], 71), 0)
    basis_output = draw_basis_output(jax.random.fold_in(arg_keys[8], 71), 0)
    return {"tokens": tokens, "segments": segments, "norm_gain": norm_gain, "q_weight": q_weight, "kv_weight": kv_weight, "o_weight": o_weight, "basis_query": basis_query, "basis_output": basis_output}


PRECISE = lax.Precision.HIGHEST
ROPE_BASE = 500000.0
NORM_EPS = 1e-05
BETA_EPS = 1e-06

def rope_tables(length, head_width):
    half_width = head_width // 2
    frequency = jnp.exp(jnp.arange(half_width, dtype=jnp.float32) * (-2.0 * math.log(ROPE_BASE) / head_width))
    angles = jnp.arange(length, dtype=jnp.float32)[:, None] * frequency[None, :]
    return (jnp.cos(angles), jnp.sin(angles))

def rotate(vectors, cosine_table, sine_table):
    half_width = vectors.shape[-1] // 2
    front_half = vectors[..., :half_width]
    back_half = vectors[..., half_width:]
    return jnp.concatenate([front_half * cosine_table - back_half * sine_table, front_half * sine_table + back_half * cosine_table], axis=-1)

def attend(query, key_states, values, allowed):
    length = query.shape[1]
    head_width = query.shape[-1]
    cosine_table, sine_table = rope_tables(length, head_width)
    query = rotate(query, cosine_table[:, None, :], sine_table[:, None, :])
    key_states = rotate(key_states, cosine_table, sine_table)
    scores = jnp.einsum('slgd,smd->sglm', query, key_states, precision=PRECISE) * head_width ** (-0.5)
    scores = jnp.where(allowed[:, None, :, :], scores, -1e+30)
    row_max = lax.stop_gradient(lax.optimization_barrier(jnp.max(scores, axis=-1, keepdims=True)))
    weights = jnp.exp(scores - row_max)
    probabilities = weights / lax.optimization_barrier(jnp.sum(weights, axis=-1, keepdims=True))
    return jnp.einsum('sglm,smd->slgd', probabilities, values, precision=PRECISE)

def allowed_pairs(segments):
    length = segments.shape[1]
    position = jnp.arange(length, dtype=jnp.int32)
    causal = position[:, None] >= position[None, :]
    return jnp.logical_and(segments[:, :, None] == segments[:, None, :], causal[None])

def rms_normed(tokens, norm_gain):
    flat_rows = tokens.reshape(-1, tokens.shape[-1]).astype(jnp.float32)
    inv_rms = lax.rsqrt(lax.optimization_barrier(jnp.mean(flat_rows * flat_rows, axis=1, keepdims=True)) + NORM_EPS)
    return (flat_rows * inv_rms * norm_gain[None, :]).astype(jnp.bfloat16)

def rounded_sum(block_term, term_count, out_shape):

    def add_term(running, block_index):
        rounded = lax.optimization_barrier(block_term(block_index).astype(jnp.bfloat16))
        return (running + rounded.astype(jnp.float32), None)
    running, _ = lax.scan(add_term, jnp.zeros(out_shape, jnp.float32), jnp.arange(term_count, dtype=jnp.int32))
    return running

def reference(tokens, segments, norm_gain, q_weight, kv_weight, o_weight, basis_query, basis_output):
    seq_count, length, model_width = tokens.shape
    qwidth = QH * HD
    group_size = QH // KVH
    row_count = seq_count * length
    block_rows = row_count // N_DP
    col_count = qwidth // N_TENSOR
    query_scale = D ** (-0.5)
    output_scale = qwidth ** (-0.5)
    gn_scale = qwidth / row_count
    param_count = 2.0 * D * qwidth
    normed = rms_normed(tokens, norm_gain)
    dir_query = basis_query[K - 1]
    dir_output = basis_output[K - 1]
    query = jnp.dot(normed, q_weight, preferred_element_type=jnp.float32).astype(jnp.bfloat16)
    tangent = (jnp.dot(normed, dir_query, preferred_element_type=jnp.float32) * query_scale).astype(jnp.bfloat16)
    key_states = jnp.dot(normed, kv_weight[0], preferred_element_type=jnp.float32).astype(jnp.bfloat16)
    values = jnp.dot(normed, kv_weight[1], preferred_element_type=jnp.float32).astype(jnp.bfloat16)
    allowed = allowed_pairs(segments)
    query_wide = query.astype(jnp.float32).reshape(seq_count, length, KVH, group_size, HD)
    tangent_wide = tangent.astype(jnp.float32).reshape(seq_count, length, KVH, group_size, HD)
    key_wide = key_states.astype(jnp.float32).reshape(seq_count, length, KVH, HD)
    value_wide = values.astype(jnp.float32).reshape(seq_count, length, KVH, HD)

    def forward(query_arg, tangent_arg, key_arg, value_arg):
        return jax.jvp(lambda moving: attend(moving, key_arg, value_arg, allowed), (query_arg,), (tangent_arg,))
    heads_out, tangent_heads = jax.vmap(forward, in_axes=(2, 2, 2, 2), out_axes=2)(query_wide, tangent_wide, key_wide, value_wide)
    heads_out = heads_out.reshape(row_count, qwidth).astype(jnp.bfloat16)
    tangent_heads = tangent_heads.reshape(row_count, qwidth).astype(jnp.bfloat16)

    def head_term(block_index):
        offset = block_index * col_count
        part_heads = lax.dynamic_slice_in_dim(heads_out, offset, col_count, 1)
        part_tangent = lax.dynamic_slice_in_dim(tangent_heads, offset, col_count, 1)
        part_dir = lax.dynamic_slice_in_dim(dir_output, offset, col_count, 0)
        part_weight = lax.dynamic_slice_in_dim(o_weight, offset, col_count, 0)
        return jnp.dot(part_heads, part_dir, preferred_element_type=jnp.float32) * output_scale + jnp.dot(part_tangent, part_weight, preferred_element_type=jnp.float32)
    tangent_out = rounded_sum(head_term, N_TENSOR, (row_count, D)).astype(jnp.bfloat16)
    cot_heads = lax.dot_general(tangent_out, o_weight, (((1,), (1,)), ((), ())), preferred_element_type=jnp.float32)
    cot_heads = cot_heads.reshape(seq_count, length, KVH, group_size, HD)

    def backward(query_arg, key_arg, value_arg, cot_arg):
        _, pullback = jax.vjp(lambda moving: attend(moving, key_arg, value_arg, allowed), query_arg)
        return pullback(cot_arg)[0]
    cot_query = jax.vmap(backward, in_axes=(2, 2, 2, 2), out_axes=2)(query_wide, key_wide, value_wide, cot_heads)
    cot_query = cot_query.reshape(row_count, qwidth).astype(jnp.bfloat16)

    def query_term(block_index):
        left_rows = lax.dynamic_slice_in_dim(normed, block_index * block_rows, block_rows, 0)
        right_rows = lax.dynamic_slice_in_dim(cot_query, block_index * block_rows, block_rows, 0)
        return lax.dot_general(left_rows, right_rows, (((0,), (0,)), ((), ())), preferred_element_type=jnp.float32) * (gn_scale * query_scale)

    def output_term(block_index):
        left_rows = lax.dynamic_slice_in_dim(heads_out, block_index * block_rows, block_rows, 0)
        right_rows = lax.dynamic_slice_in_dim(tangent_out, block_index * block_rows, block_rows, 0)
        return lax.dot_general(left_rows, right_rows, (((0,), (0,)), ((), ())), preferred_element_type=jnp.float32) * (gn_scale * output_scale)
    gn_query = rounded_sum(query_term, N_DP, (D, qwidth))
    gn_output = rounded_sum(output_term, N_DP, (qwidth, D))

    def products(vec_query, vec_output):

        def per_vector(basis_pair):
            return jnp.sum(basis_pair[0].astype(jnp.float32) * vec_query) + jnp.sum(basis_pair[1].astype(jnp.float32) * vec_output)
        return lax.map(per_vector, (basis_query, basis_output)) / param_count

    def remove(vec_query, vec_output, weights_now):

        def subtract(carried, basis_item):
            coefficient, part_query, part_output = basis_item
            return ((carried[0] - coefficient * part_query.astype(jnp.float32), carried[1] - coefficient * part_output.astype(jnp.float32)), None)
        carried, _ = lax.scan(subtract, (vec_query, vec_output), (weights_now, basis_query, basis_output))
        return carried
    first_coeffs = products(gn_query, gn_output)
    kept_query, kept_output = remove(gn_query, gn_output, first_coeffs)
    second_coeffs = products(kept_query, kept_output)
    clean_query, clean_output = remove(kept_query, kept_output, second_coeffs)
    squares = (jnp.sum(clean_query * clean_query) + jnp.sum(clean_output * clean_output)) / param_count
    beta = jnp.sqrt(squares + BETA_EPS)
    coefficients = jnp.concatenate([first_coeffs + second_coeffs, beta[None]])
    return ((clean_query / beta).astype(jnp.bfloat16), (clean_output / beta).astype(jnp.bfloat16), coefficients)
```

```python
import functools
import math

import jax
import jax.numpy as jnp
import numpy as np
from jax import lax
from jax.experimental import pallas as pl
from jax.experimental.pallas import tpu as pltpu
from jax.sharding import PartitionSpec as P


HD = 128
QH = 32
KVH = 4
ROPE_BASE = 500000.0
NORM_EPS = 1e-05
BETA_EPS = 1e-06

BF = jnp.bfloat16
F32 = jnp.float32


DOT_NN = (((1,), (0,)), ((), ()))
DOT_NT = (((1,), (1,)), ((), ()))
DOT_TN = (((0,), (0,)), ((), ()))


def mm(a, b, dims=DOT_NN):
    return lax.dot_general(a, b, dims, preferred_element_type=F32)


def split2(x):
    high = x.astype(BF)
    return high, (x - high.astype(F32)).astype(BF)


def mm3(a, b, dims=DOT_NN):
    a_high, a_low = a
    b_high, b_low = b
    return mm(a_high, b_high, dims) + (mm(a_high, b_low, dims) + mm(a_low, b_high, dims))


def cost(flops, bytes_accessed):
    return pl.CostEstimate(flops=int(flops), bytes_accessed=int(bytes_accessed), transcendentals=0)


def params(limit_mib):
    return pltpu.CompilerParams(vmem_limit_bytes=limit_mib << 20)


def in_hbm(x):
    return pltpu.with_memory_space_constraint(x, pltpu.HBM)


def rope_tables(length):
    half = HD // 2
    frequency = np.exp(
        np.arange(half, dtype=np.float32) * np.float32(-2.0 * math.log(ROPE_BASE) / HD)
    ).astype(np.float32)
    angles = np.arange(length, dtype=np.float32)[:, None] * frequency[None, :]
    cosine = np.cos(angles).astype(np.float32)
    sine = np.sin(angles).astype(np.float32)
    return (
        np.concatenate([cosine, cosine], axis=1),
        np.concatenate([-sine, sine], axis=1),
    )


def swap_halves(x):
    half = x.shape[-1] // 2
    return jnp.concatenate([x[:, half:], x[:, :half]], axis=-1)


def norm_kernel(place_ref, x_ref, gain_ref, *out_refs):
    count = len(out_refs)
    block = x_ref.shape[1] // count
    mine = place_ref[1]
    total = None
    for e in range(count):
        part = x_ref[:, e * block : (e + 1) * block].astype(F32)
        part = jnp.sum(part * part, axis=1, keepdims=True)
        total = part if total is None else total + part
    inv_rms = lax.rsqrt(total / x_ref.shape[1] + NORM_EPS)
    for r in range(count):
        offset = pl.multiple_of((mine ^ r) * block, block)
        part = x_ref[:, pl.ds(offset, block)].astype(F32)
        gain = gain_ref[:, pl.ds(offset, block)]
        out_refs[r][...] = (part * inv_rms * gain).astype(BF)


def norm_blocks(place, flat_tokens, gain, rows, count):
    width = flat_tokens.shape[1]
    block = width // count
    tile = 64
    steps = rows // tile
    return pl.pallas_call(
        norm_kernel,
        grid_spec=pltpu.PrefetchScalarGridSpec(
            num_scalar_prefetch=1,
            grid=(steps,),
            in_specs=[
                pl.BlockSpec((tile, width), lambda i, place_ref: (place_ref[0] * steps + i, 0)),
                pl.BlockSpec((1, width), lambda i, place_ref: (0, 0)),
            ],
            out_specs=[pl.BlockSpec((tile, block), lambda i, place_ref: (i, 0))] * count,
        ),
        out_shape=[jax.ShapeDtypeStruct((rows, block), BF)] * count,
        cost_estimate=cost(rows * width * 8, rows * width * 4),
        compiler_params=params(24),
        name="norm_blocks",
    )(place, in_hbm(flat_tokens), gain)


def project_kernel(scale, place_ref, mine_ref, other_ref, q_ref, t_ref, k_ref, v_ref, *outs):
    tile = q_ref.shape[1]
    step = pl.program_id(0)
    lhs = (mine_ref[...], other_ref[...])
    columns = pl.ds(pl.multiple_of(step * tile, tile), tile)
    for s in range(2):
        outs[0][s, :, columns] = mm(lhs[s], q_ref[...]).astype(BF)
        outs[1][s, :, columns] = (mm(lhs[s], t_ref[0]) * scale).astype(BF)

    @pl.when(step == 0)
    def _():
        for out_ref, weight_ref in zip(outs, (k_ref, v_ref)):
            cols = out_ref.shape[2] - HD
            for s in range(2):
                out_ref[s, :, cols:] = mm(lhs[s], weight_ref[0]).astype(BF)


def project(place, mine, other, q_weight, basis_query, kv_weight, scale):
    rows, depth = mine.shape
    cols = q_weight.shape[1]
    tile = min(256, cols)
    last = basis_query.shape[0] - 1
    whole = pl.BlockSpec((rows, depth), lambda i, place_ref: (0, 0))
    shape = (2, rows, cols + HD)
    return pl.pallas_call(
        functools.partial(project_kernel, scale),
        grid_spec=pltpu.PrefetchScalarGridSpec(
            num_scalar_prefetch=1,
            grid=(cols // tile,),
            in_specs=[
                whole,
                whole,
                pl.BlockSpec((depth, tile), lambda i, place_ref: (0, i)),
                pl.BlockSpec((1, depth, tile), lambda i, place_ref: (last, 0, i)),
                pl.BlockSpec((1, depth, HD), lambda i, place_ref: (0, 0, place_ref[2])),
                pl.BlockSpec((1, depth, HD), lambda i, place_ref: (1, 0, place_ref[2])),
            ],
            out_specs=[pl.BlockSpec(shape, lambda i, place_ref: (0, 0, 0))] * 2,
        ),
        out_shape=[jax.ShapeDtypeStruct(shape, BF)] * 2,
        cost_estimate=cost(8 * rows * depth * (cols + HD), 4 * depth * (cols + HD + rows)),
        compiler_params=params(24),
        name="project",
    )(place, mine, other, q_weight, in_hbm(basis_query), kv_weight, kv_weight)


def attend_kernel(count, heads, place_ref, *refs):
    query_parts = refs[:count]
    tangent_parts = refs[count : 2 * count]
    cos_ref, sin_ref, segment_ref = refs[2 * count : 2 * count + 3]
    whole_ref, *half_refs = refs[2 * count + 3 : 2 * count + 6]
    prob_ref, key_ref, value_ref = refs[2 * count + 6 :]
    length = cos_ref.shape[0]
    cols = heads * HD
    cosine = cos_ref[...]
    sine = sin_ref[...]

    def summed(parts, start):
        total = parts[0][0, :, start : start + HD].astype(F32)
        for part in parts[1:]:
            total = total + part[0, :, start : start + HD].astype(F32)
        return total.astype(BF)

    def turned(x):
        x = x.astype(F32)
        return x * cosine + swap_halves(x) * sine

    keys = turned(summed(query_parts, cols))
    values = summed(tangent_parts, cols)
    key_ref[0] = keys
    value_ref[0] = values
    key_pair = split2(keys)
    row = lax.broadcasted_iota(jnp.int32, (length, length), 0)
    column = lax.broadcasted_iota(jnp.int32, (length, length), 1)
    segment = jnp.where(
        (pl.program_id(0) + place_ref[0]) % 2 == 0, segment_ref[0:1], segment_ref[1:2]
    )
    segment = jnp.broadcast_to(segment.astype(F32), (length, length))
    allowed = jnp.logical_and(row >= column, segment == segment.T)
    half = length // 2
    for h in range(heads):
        query = split2(turned(summed(query_parts, h * HD)))
        tangent = split2(turned(summed(tangent_parts, h * HD)))
        scores = jnp.where(allowed, mm3(query, key_pair, DOT_NT) * HD ** (-0.5), -1e30)
        weights = jnp.exp(scores - jnp.max(scores, axis=-1, keepdims=True))
        probs = weights / jnp.sum(weights, axis=-1, keepdims=True)
        moved = mm3(tangent, key_pair, DOT_NT) * HD ** (-0.5)
        weighted = probs * moved
        moved_probs = weighted - probs * jnp.sum(weighted, axis=-1, keepdims=True)
        prob_ref[0, h] = probs
        for source, base in ((probs, 0), (moved_probs, cols)):
            high, low = split2(source)
            result = (mm(high, values) + mm(low, values)).astype(BF)
            columns = slice(base + h * HD, base + (h + 1) * HD)
            whole_ref[0, :, columns] = result
            for n in range(2):
                half_refs[n][0, :, columns] = result[n * half : (n + 1) * half]


def attend(place, query_parts, tangent_parts, segments, tables, heads):
    seqs, length, width = query_parts[0].shape
    cols = heads * HD
    one = lambda *shape: pl.BlockSpec(
        (1, *shape), lambda s, place_ref: (s,) + (0,) * len(shape)
    )
    table = pl.BlockSpec((length, HD), lambda s, place_ref: (0, 0))
    return pl.pallas_call(
        functools.partial(attend_kernel, len(query_parts), heads),
        grid_spec=pltpu.PrefetchScalarGridSpec(
            num_scalar_prefetch=1,
            grid=(seqs,),
            in_specs=[one(length, width)] * (2 * len(query_parts))
            + [table, table, pl.BlockSpec((seqs, length), lambda s, place_ref: (0, 0))],
            out_specs=[
                one(length, 2 * cols),
                one(length // 2, 2 * cols),
                one(length // 2, 2 * cols),
                one(heads, length, length),
                one(length, HD),
                one(length, HD),
            ],
        ),
        out_shape=[
            jax.ShapeDtypeStruct((seqs, length, 2 * cols), BF),
            jax.ShapeDtypeStruct((seqs, length // 2, 2 * cols), BF),
            jax.ShapeDtypeStruct((seqs, length // 2, 2 * cols), BF),
            jax.ShapeDtypeStruct((seqs, heads, length, length), F32),
            jax.ShapeDtypeStruct((seqs, length, HD), F32),
            jax.ShapeDtypeStruct((seqs, length, HD), BF),
        ],
        cost_estimate=cost(seqs * heads * length * length * HD * 24, seqs * length * width * 8),
        compiler_params=params(20),
        name="attend",
    )(place, *query_parts, *tangent_parts, *tables, segments)


def transpose_kernel(count, heads, *refs):
    parts = refs[:count]
    prob_ref, key_ref, value_ref, cos_ref, sin_ref, out_ref = refs[count:]
    key_pair = split2(key_ref[0])
    values = value_ref[0]
    cosine = cos_ref[...]
    sine = sin_ref[...]
    for h in range(heads):
        total = parts[0][0, :, h * HD : (h + 1) * HD].astype(F32)
        for part in parts[1:]:
            part = part.at[0] if len(part.shape) == 4 else part
            total = total + part[0, :, h * HD : (h + 1) * HD].astype(F32)
        high, low = split2(total)
        probs = prob_ref[0, h]
        weighted = probs * (mm(high, values, DOT_NT) + mm(low, values, DOT_NT))
        moved = weighted - probs * jnp.sum(weighted, axis=-1, keepdims=True)
        back = mm3(split2(moved), key_pair) * HD ** (-0.5)
        out_ref[0, :, h * HD : (h + 1) * HD] = (back * cosine - swap_halves(back) * sine).astype(
            BF
        )


def attend_transpose(parts, probs, keys, values, tables, heads, which):
    seqs, rows, cols = parts[0].shape
    length = keys.shape[1]
    one = lambda *shape: pl.BlockSpec((1, *shape), lambda s: (s,) + (0,) * len(shape))
    table = pl.BlockSpec((rows, HD), lambda s: (which, 0))
    return pl.pallas_call(
        functools.partial(transpose_kernel, len(parts), heads),
        grid=(seqs,),
        in_specs=[
            one(rows, cols)
            if part.ndim == 3
            else pl.BlockSpec((1, 1, rows, cols), lambda s: (which, s, 0, 0))
            for part in parts
        ]
        + [
            pl.BlockSpec((1, heads, rows, length), lambda s: (s, 0, which, 0)),
            one(length, HD),
            one(length, HD),
            table,
            table,
        ],
        out_specs=one(rows, cols),
        out_shape=jax.ShapeDtypeStruct((seqs, rows, cols), BF),
        cost_estimate=cost(seqs * heads * rows * length * HD * 10, seqs * rows * cols * 16),
        compiler_params=params(16),
        name="attend_transpose",
    )(*parts, probs, keys, values, *tables)


def fold(x):
    rows, width = x.shape
    x = jnp.sum(x.reshape(rows // 8, 8, width), axis=0)
    total = x[:, :128]
    for start in range(128, width, 128):
        total = total + x[:, start : start + 128]
    return total


def add_products(sums_ref, basis_ref, g, first):
    stored = basis_ref.shape[0]

    @pl.when(first)
    def _():
        sums_ref[...] = jnp.zeros_like(sums_ref)

    for j in range(stored):
        sums_ref[j] += fold(basis_ref[j].astype(F32) * g)
    sums_ref[stored] += fold(g * g)


def place_products(tile_ref, sums_ref, stored):
    row = lax.broadcasted_iota(jnp.int32, (stored, 128), 0)
    lane = lax.broadcasted_iota(jnp.int32, (stored, 128), 1)
    tile = jnp.zeros((stored, 128), F32)
    for j in range(stored):
        tile = jnp.where((row == j) & (lane == 0), jnp.sum(sums_ref[j], keepdims=True), tile)
    tile = jnp.where((row == 0) & (lane == 1), jnp.sum(sums_ref[stored], keepdims=True), tile)
    tile_ref[...] = tile


def gn_query_kernel(count, scale, *refs):
    mine = refs[:count]
    other = refs[count : 2 * count]
    cots = refs[2 * count : 4 * count]
    basis_ref, out_ref, tile_ref, cot_ref, sums_ref = refs[4 * count :]
    half = cots[0].shape[1]
    step = pl.program_id(0)

    @pl.when(step == 0)
    def _():
        for r in range(count):
            for n in range(2):
                for s in range(2):
                    cot_ref[r, s, n * half : (n + 1) * half] = cots[2 * r + n][s]

    total = None
    for r in range(count):
        term = mm(mine[r][...], cot_ref[r, 0], DOT_TN) + mm(other[r][...], cot_ref[r, 1], DOT_TN)
        term = (term * scale).astype(BF).astype(F32)
        total = term if total is None else total + term
    out_ref[...] = total
    add_products(sums_ref, basis_ref, total, step == 0)

    @pl.when(step == pl.num_programs(0) - 1)
    def _():
        place_products(tile_ref, sums_ref, basis_ref.shape[0])


def gn_query_products(mine, other, cots, basis, scale):
    count = len(mine)
    rows, depth = mine[0].shape
    cols = cots[0].shape[2]
    stored = basis.shape[0]
    tile = 512
    lhs = pl.BlockSpec((rows, tile), lambda i: (0, i))
    whole = pl.BlockSpec(cots[0].shape, lambda i: (0, 0, 0))
    return pl.pallas_call(
        functools.partial(gn_query_kernel, count, scale),
        grid=(depth // tile,),
        in_specs=[lhs] * (2 * count)
        + [whole] * (2 * count)
        + [pl.BlockSpec((stored, tile, cols), lambda i: (0, i, 0))],
        out_specs=[
            pl.BlockSpec((tile, cols), lambda i: (i, 0)),
            pl.BlockSpec((stored, 128), lambda i: (0, 0)),
        ],
        out_shape=[
            jax.ShapeDtypeStruct((depth, cols), F32),
            jax.ShapeDtypeStruct((stored, 128), F32),
        ],
        scratch_shapes=[
            pltpu.VMEM((count, 2, rows, cols), BF),
            pltpu.VMEM((stored + 1, 8, 128), F32),
        ],
        cost_estimate=cost(
            4 * count * rows * depth * cols, 2 * depth * (stored * cols + 2 * count * rows)
        ),
        compiler_params=params(40),
        name="gn_query_products",
    )(*mine, *other, *cots, in_hbm(basis))


def gn_output_kernel(count, scale, last, *refs):
    hts = refs[: 2 * count]
    outs = refs[2 * count : 6 * count]
    if last:
        before_ref, basis_ref, out_ref, tile_ref, head_ref, sums_ref = refs[6 * count :]
    else:
        out_ref, head_ref = refs[6 * count :]
    cols = head_ref.shape[1]
    step = pl.program_id(0)

    @pl.when(step == 0)
    def _():
        for m in range(2 * count):
            block = jnp.concatenate([hts[m][0, :, :cols], hts[m][1, :, :cols]], axis=0)
            head_ref[m] = block.T

    total = before_ref[...] if last else None
    for r in range(count):
        term = None
        for m in (2 * r, 2 * r + 1):
            both = jnp.concatenate([outs[2 * m][...], outs[2 * m + 1][...]], axis=0)
            product = mm(head_ref[m], both)
            term = product if term is None else term + product
        term = (term * scale).astype(BF).astype(F32)
        total = term if total is None else total + term
    out_ref[...] = total
    if last:
        add_products(sums_ref, basis_ref, total, step == 0)

        @pl.when(step == pl.num_programs(0) - 1)
        def _():
            place_products(tile_ref, sums_ref, basis_ref.shape[0])


def gn_output_sum(hts, halves, outs, scale, before=None, basis=None):
    count = len(hts) // 2
    rows, depth = 2 * outs[0].shape[0], outs[0].shape[1]
    cols = hts[0].shape[2] // 2
    tile = 512
    last = basis is not None
    column = pl.BlockSpec((cols, tile), lambda i: (0, i))
    in_specs = [
        pl.BlockSpec((2, rows // 2, ht.shape[2]), lambda i, n=n: (0, n, 0))
        for ht, n in zip(hts, halves)
    ]
    in_specs += [pl.BlockSpec((rows // 2, tile), lambda i: (0, i))] * (4 * count)
    out_specs = [column]
    out_shape = [jax.ShapeDtypeStruct((cols, depth), F32)]
    scratch_shapes = [pltpu.VMEM((2 * count, cols, rows), BF)]
    operands = [*hts, *outs]
    flops, moved = 4 * count * rows * depth * cols, 4 * depth * (cols + count * rows)
    if last:
        stored = basis.shape[0]
        in_specs += [column, pl.BlockSpec((stored, cols, tile), lambda i: (0, 0, i))]
        out_specs.append(pl.BlockSpec((stored, 128), lambda i: (0, 0)))
        out_shape.append(jax.ShapeDtypeStruct((stored, 128), F32))
        scratch_shapes.append(pltpu.VMEM((stored + 1, 8, 128), F32))
        operands += [before, in_hbm(basis)]
        moved += 2 * basis.size + 4 * depth * cols
    return pl.pallas_call(
        functools.partial(gn_output_kernel, count, scale, last),
        grid=(depth // tile,),
        in_specs=in_specs,
        out_specs=out_specs,
        out_shape=out_shape,
        scratch_shapes=scratch_shapes,
        cost_estimate=cost(flops, moved),
        compiler_params=params(32),
        name="gn_output_last" if last else "gn_output_first",
    )(*operands)


GRAM_ROWS = 32


def gram_kernel(basis_ref, tile_ref, total_ref):
    stored, rows, width = basis_ref.shape
    size = stored * GRAM_ROWS
    step = pl.program_id(0)

    @pl.when(step == 0)
    def _():
        total_ref[...] = jnp.zeros_like(total_ref)

    total = None
    for n in range(rows // GRAM_ROWS):
        block = basis_ref[:, n * GRAM_ROWS : (n + 1) * GRAM_ROWS, :].reshape(size, width)
        product = mm(block, block, DOT_NT)
        total = product if total is None else total + product
    total_ref[...] += total

    @pl.when(step == pl.num_programs(0) - 1)
    def _():
        row = lax.broadcasted_iota(jnp.int32, (size, size), 0)
        column = lax.broadcasted_iota(jnp.int32, (size, size), 1)
        same = jnp.where(row % GRAM_ROWS == column % GRAM_ROWS, total_ref[...], 0.0)
        sums = jnp.concatenate(
            [
                jnp.sum(same[j * GRAM_ROWS : (j + 1) * GRAM_ROWS], axis=0, keepdims=True)
                for j in range(stored)
            ],
            axis=0,
        )
        member = lax.broadcasted_iota(jnp.int32, (stored, size), 1) // GRAM_ROWS
        lane = lax.broadcasted_iota(jnp.int32, (stored, 128), 1)
        tile = jnp.zeros((stored, 128), F32)
        for k in range(stored):
            one = jnp.sum(jnp.where(member == k, sums, 0.0), axis=1, keepdims=True)
            tile = jnp.where(lane == 8 + k, one, tile)
        tile_ref[...] = tile


def basis_specs(basis_query, steps):
    stored, depth, cols = basis_query.shape
    return [
        pl.BlockSpec((stored, depth // steps, cols), lambda i: (0, i, 0)),
        pl.BlockSpec((stored, cols // steps, depth), lambda i: (0, i, 0)),
    ]


def gram(basis):
    stored, rows, width = basis.shape
    steps = 4
    size = stored * GRAM_ROWS
    return pl.pallas_call(
        gram_kernel,
        grid=(steps,),
        in_specs=[pl.BlockSpec((stored, rows // steps, width), lambda i: (0, i, 0))],
        out_specs=pl.BlockSpec((stored, 128), lambda i: (0, 0)),
        out_shape=jax.ShapeDtypeStruct((stored, 128), F32),
        scratch_shapes=[pltpu.VMEM((size, size), F32)],
        cost_estimate=cost(2 * size * basis.size, 2 * basis.size),
        compiler_params=params(20),
        name="gram",
    )(in_hbm(basis))


def clean_kernel(
    param_count, sums_ref, bq_ref, bo_ref, gq_ref, go_ref, nq_ref, no_ref, tile_ref, scalar_ref
):
    stored = bq_ref.shape[0]

    @pl.when(pl.program_id(0) == 0)
    def _():
        sums = sums_ref[...] / param_count
        first = sums[:, 0:1]
        norm = sums[0:1, 1:2]

        def times_gram(x):
            total = sums[:, 8:9] * x[0:1]
            for k in range(1, stored):
                total = total + sums[:, 8 + k : 9 + k] * x[k : k + 1]
            return total

        coeffs = first + (first - times_gram(first))
        change = jnp.sum(coeffs * (times_gram(coeffs) - 2.0 * first), axis=0, keepdims=True)
        beta = jnp.sqrt(jnp.maximum(norm + change, 0.0) + BETA_EPS)
        lane = lax.broadcasted_iota(jnp.int32, (1, 128), 1)
        tile = jnp.broadcast_to(beta, (1, 128))
        for j in range(stored):
            scalar_ref[j] = jnp.sum(coeffs[j : j + 1])
            tile = jnp.where(lane == j, coeffs[j : j + 1], tile)
        scalar_ref[stored] = jnp.sum(1.0 / beta)
        tile_ref[...] = tile

    inverse = scalar_ref[stored]
    coeffs = [scalar_ref[j] for j in range(stored)]
    for basis_ref, g_ref, next_ref in ((bq_ref, gq_ref, nq_ref), (bo_ref, go_ref, no_ref)):
        rows, width = g_ref.shape
        lanes = min(512, width)
        strips = width // lanes

        def one(n, _, basis_ref=basis_ref, g_ref=g_ref, next_ref=next_ref, strips=strips):
            row = pl.ds(pl.multiple_of((n // strips) * 16, 16), 16)
            column = pl.ds(pl.multiple_of((n % strips) * lanes, lanes), lanes)
            total = g_ref[row, column]
            for j in range(stored):
                total = total - coeffs[j] * basis_ref[j, row, column].astype(F32)
            next_ref[row, column] = (total * inverse).astype(BF)
            return 0

        lax.fori_loop(0, rows // 16 * strips, one, 0, unroll=4)


def clean(sums, basis_query, basis_output, gn_query, gn_output, param_count):
    stored, depth, cols = basis_query.shape
    steps = 8
    query_spec = pl.BlockSpec((depth // steps, cols), lambda i: (i, 0))
    output_spec = pl.BlockSpec((cols // steps, depth), lambda i: (i, 0))
    return pl.pallas_call(
        functools.partial(clean_kernel, param_count),
        grid=(steps,),
        in_specs=[pl.BlockSpec((stored, 128), lambda i: (0, 0))]
        + basis_specs(basis_query, steps)
        + [query_spec, output_spec],
        out_specs=[query_spec, output_spec, pl.BlockSpec((1, 128), lambda i: (0, 0))],
        out_shape=[
            jax.ShapeDtypeStruct((depth, cols), BF),
            jax.ShapeDtypeStruct((cols, depth), BF),
            jax.ShapeDtypeStruct((1, 128), F32),
        ],
        scratch_shapes=[pltpu.SMEM((2 * stored,), F32)],
        cost_estimate=cost(40 * depth * cols, 52 * depth * cols),
        compiler_params=params(40),
        name="clean",
    )(sums, in_hbm(basis_query), in_hbm(basis_output), gn_query, gn_output)


def right_kernel(scale, dir_ref, weight_ref, out_ref):
    out_ref[0] = (dir_ref[0].astype(F32) * scale).astype(BF)
    out_ref[1] = weight_ref[...]


def right_operand(basis, weight, scale):
    last = basis.shape[0] - 1
    cols, depth = weight.shape
    steps = 4
    tile = cols // steps
    out = pl.pallas_call(
        functools.partial(right_kernel, scale),
        grid=(steps,),
        in_specs=[
            pl.BlockSpec((1, tile, depth), lambda i: (last, i, 0)),
            pl.BlockSpec((tile, depth), lambda i: (i, 0)),
        ],
        out_specs=pl.BlockSpec((2, tile, depth), lambda i: (0, i, 0)),
        out_shape=jax.ShapeDtypeStruct((2, cols, depth), BF),
        cost_estimate=cost(cols * depth, 8 * cols * depth),
        compiler_params=params(12),
        name="right_operand",
    )(in_hbm(basis), weight)
    return out.reshape(2 * cols, depth)


def exchange(x, axis, r):
    return lax.ppermute(x, axis, [(i, i ^ r) for i in range(lax.axis_size(axis))])


def line_pairs(links):
    return [(2 * a + core, 2 * b + core) for a, b in links for core in range(2)]


def line_move(x, links):
    return lax.ppermute(x, "tensor", line_pairs(links))


def line_links():
    chips = lax.axis_size("tensor") // 2
    return [((s, s + 1), (chips - 1 - s, chips - 2 - s)) for s in range(chips // 2 - 1)]


def line_sum(x, taken):
    chips = lax.axis_size("tensor") // 2

    def add(a, b):
        return (a.astype(F32) + b.astype(F32)).astype(BF)

    inward = line_links()
    for pair in inward:
        x = add(x, line_move(x, pair))
    middle = ((chips // 2 - 1, chips // 2), (chips // 2, chips // 2 - 1))
    x = add(x, line_move(x, middle))
    for s, ((low, low_next), (high, high_next)) in reversed(list(enumerate(inward))):
        back = line_move(x, ((low_next, low), (high_next, high)))
        x = jnp.where(taken[s], back, x)
    return x


def sum_everywhere(x):
    steps = [("tensor", 1)]
    for axis, start in (("dp", 1), ("tensor", 2)):
        r = start
        while r < lax.axis_size(axis):
            steps.append((axis, r))
            r *= 2
    for axis, r in steps:
        x = x + exchange(x, axis, r)
    return x


def step(tokens, segments, norm_gain, q_weight, kv_weight, o_weight, basis_query, basis_output):
    groups = lax.axis_size("dp")
    seqs, length, width = tokens.shape
    cols = q_weight.shape[1]
    heads = cols // HD
    stored = basis_query.shape[0]
    qwidth = cols * lax.axis_size("tensor")
    query_scale = width ** (-0.5)
    output_scale = qwidth ** (-0.5)
    gn_scale = qwidth / (seqs * length * groups)
    param_count = 2.0 * width * qwidth
    rows = seqs // 2 * length
    assert seqs == 2
    dp = lax.axis_index("dp")
    tensor = lax.axis_index("tensor")
    kv_head = lax.div(tensor * heads, QH // KVH)
    place = jnp.stack([tensor & 1, dp, kv_head]).astype(jnp.int32)
    chip = tensor >> 1
    taken = [(chip == low) | (chip == high) for (low, _), (high, _) in line_links()]
    place, taken = lax.optimization_barrier((place, taken))
    tables = tuple(jnp.asarray(x) for x in rope_tables(length))

    normed = norm_blocks(
        place, tokens.reshape(seqs * length, width), norm_gain[None, :], rows, groups
    )
    mine = [normed[0]] + [exchange(normed[r], "dp", r) for r in range(1, groups)]
    other = [exchange(x, "tensor", 1) for x in mine]
    query_parts, tangent_parts = [], []
    for r in range(groups):
        query_part, tangent_part = project(
            place, mine[r], other[r], q_weight, basis_query, kv_weight, query_scale
        )
        query_parts.append(query_part)
        tangent_parts.append(tangent_part)
    bits = [1 << n for n in range(groups.bit_length() - 1)]
    query_parts = halving(query_parts, bits)
    tangent_parts = halving(tangent_parts, bits[::-1])
    ht, ht0, ht1, probs, keys, values = attend(
        place, query_parts, tangent_parts, segments, tables, heads
    )

    grams = []
    for basis in (basis_query, basis_output):
        grams.append(gram(basis))

    right = right_operand(basis_output, o_weight, output_scale)
    hts = [[(ht0, 0), (ht1, 0)], [(exchange(x, "dp", 1), 0) for x in (ht0, ht1)]]
    for r in range(2, groups):
        moved = exchange(ht, "dp", r)
        hts.append([(moved, 0), (moved, 1)])
    outs = [[None, None] for _ in range(groups)]
    cots = [[None, None] for _ in range(groups)]
    half = length // 2
    for r, n in chunk_order(groups):
        ht_now, part = hts[r][n]
        ht_rows = ht_now[:, part * half : (part + 1) * half]
        given = mm(ht_rows[1], right).astype(BF)
        given = exchange(given, "tensor", 1)
        kept = (mm(ht_rows[0], right) + given.astype(F32)).astype(BF)
        kept = line_sum(kept, taken)
        swapped = exchange(kept, "tensor", 1)
        outs[r][n] = (kept, swapped)
        out = jnp.concatenate([kept, swapped], axis=0)
        cots[r][n] = mm(out, o_weight, DOT_NT).astype(BF).reshape(2, half, cols)
    cot_moved = [exchange(jnp.stack(cots[1]), "dp", 1)]
    cot_halves = [[exchange(cots[r][n], "dp", r) for r in range(2, groups)] for n in range(2)]

    back = []
    for n in range(2):
        cot_query = attend_transpose(
            [cots[0][n], *cot_halves[n], *cot_moved], probs, keys, values, tables, heads, n
        )
        back.append([cot_query] + [exchange(cot_query, "dp", r) for r in range(1, groups)])

    def output_sum(blocks, **rest):
        pieces = [hts[r][n] for r in blocks for n in range(2)]
        return gn_output_sum(
            [x for x, _ in pieces],
            [n for _, n in pieces],
            [x for r in blocks for n in range(2) for x in outs[r][n]],
            gn_scale * output_scale,
            **rest,
        )

    (before,) = output_sum(range(1, groups - 1))
    gn_output, output_tile = output_sum([groups - 1, 0], before=before, basis=basis_output)
    gn_query, query_tile = gn_query_products(
        mine,
        other,
        [back[n][r] for r in range(groups) for n in range(2)],
        basis_query,
        gn_scale * query_scale,
    )
    sums = sum_everywhere(query_tile + (output_tile + (grams[0] + grams[1])))
    next_query, next_output, tile = clean(
        sums, basis_query, basis_output, gn_query, gn_output, param_count
    )
    return next_query, next_output, tile[0, : stored + 1]


def halving(parts, bits):
    parts = dict(enumerate(parts))
    own = [parts[0]]
    for bit in bits:
        for r in sorted(parts, reverse=True):
            if r & bit:
                moved = exchange(parts.pop(r), "dp", bit)
                if r == bit:
                    own.append(moved)
                else:
                    kept = parts[r ^ bit]
                    parts[r ^ bit] = (kept.astype(F32) + moved.astype(F32)).astype(BF)
    return own


def chunk_order(groups):
    return [(0, 0)] + [(r, n) for r in range(1, groups) for n in range(2)] + [(0, 1)]


def solution(mesh):
    return jax.shard_map(
        step,
        mesh=mesh,
        in_specs=(
            P("dp", None, None),
            P("dp", None),
            P(),
            P("dp", "tensor"),
            P(None, "dp", None),
            P("tensor", "dp"),
            P(None, "dp", "tensor"),
            P(None, "tensor", "dp"),
        ),
        out_specs=(P("dp", "tensor"), P("tensor", "dp"), P()),
        check_vma=False,
    )
```

```python
import functools
import math

import jax
import jax.numpy as jnp
import numpy as np
from jax import lax
from jax.experimental import pallas as pl
from jax.experimental.pallas import tpu as pltpu
from jax.sharding import PartitionSpec as P


HD = 128
QH = 32
KVH = 4
ROPE_BASE = 500000.0
NORM_EPS = 1e-05
BETA_EPS = 1e-06

BF = jnp.bfloat16
F32 = jnp.float32


DOT_NN = (((1,), (0,)), ((), ()))
DOT_NT = (((1,), (1,)), ((), ()))
DOT_TN = (((0,), (0,)), ((), ()))


def mm(a, b, dims=DOT_NN):
    return lax.dot_general(a, b, dims, preferred_element_type=F32)


def split2(x):
    high = x.astype(BF)
    return high, (x - high.astype(F32)).astype(BF)


def mm3(a, b, dims=DOT_NN):
    a_high, a_low = a
    b_high, b_low = b
    return mm(a_high, b_high, dims) + (mm(a_high, b_low, dims) + mm(a_low, b_high, dims))


def cost(flops, bytes_accessed):
    return pl.CostEstimate(flops=int(flops), bytes_accessed=int(bytes_accessed), transcendentals=0)


def params(limit_mib):
    return pltpu.CompilerParams(vmem_limit_bytes=limit_mib << 20)


def in_hbm(x):
    return pltpu.with_memory_space_constraint(x, pltpu.HBM)


def rope_tables(length):
    half = HD // 2
    frequency = np.exp(
        np.arange(half, dtype=np.float32) * np.float32(-2.0 * math.log(ROPE_BASE) / HD)
    ).astype(np.float32)
    angles = np.arange(length, dtype=np.float32)[:, None] * frequency[None, :]
    cosine = np.cos(angles).astype(np.float32)
    sine = np.sin(angles).astype(np.float32)
    return np.concatenate([cosine, sine], axis=1)


def table_pair(table):
    half = table.shape[1] // 2
    cosine, sine = table[:, :half], table[:, half:]
    return jnp.concatenate([cosine, cosine], axis=1), jnp.concatenate([-sine, sine], axis=1)


def swap_halves(x):
    half = x.shape[-1] // 2
    return jnp.concatenate([x[:, half:], x[:, :half]], axis=-1)


ROWS = 32


def norm_kernel(groups, place_ref, x_ref, gain_ref, *out_refs):
    block = x_ref.shape[1] // groups
    mine = place_ref[1]
    total = None
    for e in range(groups):
        part = x_ref[:, e * block : (e + 1) * block].astype(F32)
        part = jnp.sum(part * part, axis=1, keepdims=True)
        total = part if total is None else total + part
    inv_rms = lax.rsqrt(total / x_ref.shape[1] + NORM_EPS)
    for r, out_ref in enumerate(out_refs):
        offset = pl.multiple_of((mine ^ r) * block, block)
        part = x_ref[:, pl.ds(offset, block)].astype(F32)
        gain = gain_ref[:, pl.ds(offset, block)]
        out_ref[...] = (part * inv_rms * gain).astype(BF)


def norm_blocks(place, flat_tokens, gain, rows, which, groups, count):
    width = flat_tokens.shape[1]
    block = width // groups
    steps = rows // ROWS
    half = flat_tokens.shape[0] // (2 * ROWS)
    return pl.pallas_call(
        functools.partial(norm_kernel, groups),
        grid_spec=pltpu.PrefetchScalarGridSpec(
            num_scalar_prefetch=1,
            grid=(steps,),
            in_specs=[
                pl.BlockSpec(
                    (ROWS, width),
                    lambda i, place_ref: (place_ref[0] * half + place_ref[which] + i, 0),
                ),
                pl.BlockSpec((1, width), lambda i, place_ref: (0, 0)),
            ],
            out_specs=[pl.BlockSpec((ROWS, block), lambda i, place_ref: (i, 0))] * count,
        ),
        out_shape=[jax.ShapeDtypeStruct((rows, block), BF)] * count,
        cost_estimate=cost(rows * width * 8, rows * width * 4),
        compiler_params=params(24),
        name="norm_blocks",
    )(place, in_hbm(flat_tokens), gain)


def piece_offsets(place_ref, rows):
    low, high = place_ref[3] * ROWS, place_ref[5] * ROWS
    return (
        (pl.multiple_of(low, ROWS), rows * 3 // 8),
        (rows * 3 // 8, rows // 4),
        (pl.multiple_of(high, ROWS), rows * 3 // 8),
    )


def project_kernel(scale, place_ref, *refs):
    mine, other = refs[:3], refs[3:6]
    q_ref, t_ref, k_ref, v_ref = refs[6:10]
    outs = refs[10:]
    tile = q_ref.shape[1]
    step = pl.program_id(0)
    columns = pl.ds(pl.multiple_of(step * tile, tile), tile)
    pieces = piece_offsets(place_ref, outs[0].shape[1])

    def over(columns, triples):
        for (offset, size), mine_ref, other_ref in zip(pieces, mine, other):
            rows = pl.ds(offset, size)
            both = jnp.concatenate([mine_ref[...], other_ref[...]], axis=0)
            for out_ref, weight, factor in triples:
                product = mm(both, weight())
                product = (product if factor is None else product * factor).astype(BF)
                out_ref[0, rows, columns] = product[:size]
                out_ref[1, rows, columns] = product[size:]

    over(
        columns,
        ((outs[0], lambda: q_ref[...], None), (outs[1], lambda: t_ref[0], scale)),
    )

    @pl.when(step == 0)
    def _():
        last = slice(outs[0].shape[2] - HD, outs[0].shape[2])
        over(last, ((outs[0], lambda: k_ref[0], None), (outs[1], lambda: v_ref[0], None)))


def project(place, mine, other, q_weight, basis_query, kv_weight, scale):
    rows, depth = sum(x.shape[0] for x in mine), mine[0].shape[1]
    cols = q_weight.shape[1]
    tile = min(256, cols)
    last = basis_query.shape[0] - 1
    shape = (2, rows, cols + HD)
    return pl.pallas_call(
        functools.partial(project_kernel, scale),
        grid_spec=pltpu.PrefetchScalarGridSpec(
            num_scalar_prefetch=1,
            grid=(cols // tile,),
            in_specs=[
                pl.BlockSpec(x.shape, lambda i, place_ref: (0, 0)) for x in (*mine, *other)
            ]
            + [
                pl.BlockSpec((depth, tile), lambda i, place_ref: (0, i)),
                pl.BlockSpec((1, depth, tile), lambda i, place_ref: (last, 0, i)),
                pl.BlockSpec((1, depth, HD), lambda i, place_ref: (0, 0, place_ref[2])),
                pl.BlockSpec((1, depth, HD), lambda i, place_ref: (1, 0, place_ref[2])),
            ],
            out_specs=[pl.BlockSpec(shape, lambda i, place_ref: (0, 0, 0))] * 2,
        ),
        out_shape=[jax.ShapeDtypeStruct(shape, BF)] * 2,
        cost_estimate=cost(8 * rows * depth * (cols + HD), 4 * depth * (cols + HD + rows)),
        compiler_params=params(24),
        name="project",
    )(place, *mine, *other, q_weight, in_hbm(basis_query), kv_weight, kv_weight)


def attend_kernel(count, heads, place_ref, *refs):
    query_parts = refs[:count]
    tangent_parts = refs[count : 2 * count]
    table_ref, segment_ref = refs[2 * count : 2 * count + 2]
    whole_ref, *half_refs = refs[2 * count + 2 : 2 * count + 5]
    prob_ref, key_ref, value_ref = refs[2 * count + 5 :]
    length = table_ref.shape[0]
    cols = heads * HD
    cosine, sine = table_pair(table_ref[...])

    def summed(parts, start):
        columns = pl.ds(pl.multiple_of(start, HD), HD)
        total = parts[0][0, :, columns].astype(F32)
        for part in parts[1:]:
            total = total + part[0, :, columns].astype(F32)
        return total.astype(BF)

    def turned(x):
        x = x.astype(F32)
        return x * cosine + swap_halves(x) * sine

    keys = turned(summed(query_parts, cols))
    values = summed(tangent_parts, cols)
    key_ref[0] = keys
    value_ref[0] = values
    key_pair = split2(keys)
    row = lax.broadcasted_iota(jnp.int32, (length, length), 0)
    column = lax.broadcasted_iota(jnp.int32, (length, length), 1)
    segment = jnp.where(
        (pl.program_id(0) + place_ref[0]) % 2 == 0, segment_ref[0:1], segment_ref[1:2]
    )
    segment = jnp.broadcast_to(segment.astype(F32), (length, length))
    allowed = jnp.logical_and(row >= column, segment == segment.T)
    half = length // 2

    def one(h, _):
        query = split2(turned(summed(query_parts, h * HD)))
        tangent = split2(turned(summed(tangent_parts, h * HD)))
        scores = jnp.where(allowed, mm3(query, key_pair, DOT_NT) * HD ** (-0.5), -1e30)
        weights = jnp.exp(scores - jnp.max(scores, axis=-1, keepdims=True))
        probs = weights / jnp.sum(weights, axis=-1, keepdims=True)
        moved = mm3(tangent, key_pair, DOT_NT) * HD ** (-0.5)
        weighted = probs * moved
        moved_probs = weighted - probs * jnp.sum(weighted, axis=-1, keepdims=True)
        prob_ref[0, h] = probs
        for source, base in ((probs, 0), (moved_probs, cols)):
            high, low = split2(source)
            result = (mm(high, values) + mm(low, values)).astype(BF)
            columns = pl.ds(pl.multiple_of(base + h * HD, HD), HD)
            whole_ref[0, :, columns] = result
            for n in range(2):
                half_refs[n][0, :, columns] = result[n * half : (n + 1) * half]
        return 0

    lax.fori_loop(0, heads, one, 0, unroll=2)


def attend(place, query_parts, tangent_parts, segments, table, heads):
    seqs, length, width = query_parts[0].shape
    cols = heads * HD
    one = lambda *shape: pl.BlockSpec(
        (1, *shape), lambda s, place_ref: (s,) + (0,) * len(shape)
    )
    table_spec = pl.BlockSpec((length, HD), lambda s, place_ref: (0, 0))
    return pl.pallas_call(
        functools.partial(attend_kernel, len(query_parts), heads),
        grid_spec=pltpu.PrefetchScalarGridSpec(
            num_scalar_prefetch=1,
            grid=(seqs,),
            in_specs=[one(length, width)] * (2 * len(query_parts))
            + [table_spec, pl.BlockSpec((seqs, length), lambda s, place_ref: (0, 0))],
            out_specs=[
                one(length, 2 * cols),
                one(length // 2, 2 * cols),
                one(length // 2, 2 * cols),
                one(heads, length, length),
                one(length, HD),
                one(length, HD),
            ],
        ),
        out_shape=[
            jax.ShapeDtypeStruct((seqs, length, 2 * cols), BF),
            jax.ShapeDtypeStruct((seqs, length // 2, 2 * cols), BF),
            jax.ShapeDtypeStruct((seqs, length // 2, 2 * cols), BF),
            jax.ShapeDtypeStruct((seqs, heads, length, length), F32),
            jax.ShapeDtypeStruct((seqs, length, HD), F32),
            jax.ShapeDtypeStruct((seqs, length, HD), BF),
        ],
        cost_estimate=cost(seqs * heads * length * length * HD * 24, seqs * length * width * 8),
        compiler_params=params(20),
        name="attend",
    )(place, *query_parts, *tangent_parts, table, segments)


def transpose_kernel(count, heads, *refs):
    parts = refs[:count]
    prob_ref, key_ref, value_ref, table_ref, out_ref = refs[count:]
    key_pair = split2(key_ref[0])
    values = value_ref[0]
    cosine, sine = table_pair(table_ref[...])

    def one(h, _):
        columns = pl.ds(pl.multiple_of(h * HD, HD), HD)
        total = parts[0][0, :, columns].astype(F32)
        for part in parts[1:]:
            part = part.at[0] if len(part.shape) == 4 else part
            total = total + part[0, :, columns].astype(F32)
        high, low = split2(total)
        probs = prob_ref[0, h]
        weighted = probs * (mm(high, values, DOT_NT) + mm(low, values, DOT_NT))
        moved = weighted - probs * jnp.sum(weighted, axis=-1, keepdims=True)
        back = mm3(split2(moved), key_pair) * HD ** (-0.5)
        out_ref[0, :, columns] = (back * cosine - swap_halves(back) * sine).astype(BF)
        return 0

    lax.fori_loop(0, heads, one, 0, unroll=2)


def attend_transpose(parts, probs, keys, values, table, heads, which):
    seqs, rows, cols = parts[0].shape
    length = keys.shape[1]
    one = lambda *shape: pl.BlockSpec((1, *shape), lambda s: (s,) + (0,) * len(shape))
    table_spec = pl.BlockSpec((rows, HD), lambda s: (which, 0))
    return pl.pallas_call(
        functools.partial(transpose_kernel, len(parts), heads),
        grid=(seqs,),
        in_specs=[
            one(rows, cols)
            if part.ndim == 3
            else pl.BlockSpec((1, 1, rows, cols), lambda s: (which, s, 0, 0))
            for part in parts
        ]
        + [
            pl.BlockSpec((1, heads, rows, length), lambda s: (s, 0, which, 0)),
            one(length, HD),
            one(length, HD),
            table_spec,
        ],
        out_specs=one(rows, cols),
        out_shape=jax.ShapeDtypeStruct((seqs, rows, cols), BF),
        cost_estimate=cost(seqs * heads * rows * length * HD * 10, seqs * rows * cols * 16),
        compiler_params=params(16),
        name="attend_transpose",
    )(*parts, probs, keys, values, table)


def fold(x):
    rows, width = x.shape
    x = jnp.sum(x.reshape(rows // 8, 8, width), axis=0)
    total = x[:, :128]
    for start in range(128, width, 128):
        total = total + x[:, start : start + 128]
    return total


STRIP = 256


def clear_products(sums_ref, first):
    @pl.when(first)
    def _():
        sums_ref[...] = jnp.zeros_like(sums_ref)


def add_products(sums_ref, basis_ref, g):
    stored = basis_ref.shape[0]
    for j in range(stored):
        sums_ref[j] += fold(basis_ref[j].astype(F32) * g)
    sums_ref[stored] += fold(g * g)


def place_products(tile_ref, sums_ref, stored):
    row = lax.broadcasted_iota(jnp.int32, (stored, 128), 0)
    lane = lax.broadcasted_iota(jnp.int32, (stored, 128), 1)
    tile = jnp.zeros((stored, 128), F32)
    for j in range(stored):
        tile = jnp.where((row == j) & (lane == 0), jnp.sum(sums_ref[j], keepdims=True), tile)
    tile = jnp.where((row == 0) & (lane == 1), jnp.sum(sums_ref[stored], keepdims=True), tile)
    tile_ref[...] = tile


def gn_query_kernel(count, scale, place_ref, *refs):
    mine = [refs[3 * r : 3 * r + 3] for r in range(count)]
    other = [refs[3 * (count + r) : 3 * (count + r) + 3] for r in range(count)]
    cots = refs[6 * count : 8 * count]
    basis_ref, out_ref, tile_ref, plain_ref, cot_ref, sums_ref = refs[8 * count :]
    half = cots[0].shape[1]
    step = pl.program_id(0)

    @pl.when(step == 0)
    def _():
        for r in range(count):
            for s in range(2):
                for n in range(2):
                    plain_ref[n * half : (n + 1) * half] = cots[2 * r + n][s]
                start = 0
                for offset, size in piece_offsets(place_ref, 2 * half):
                    cot_ref[r, s, start : start + size] = plain_ref[pl.ds(offset, size), :]
                    start += size

    clear_products(sums_ref, step == 0)

    def one(n, _):
        rows = pl.ds(pl.multiple_of(n * STRIP, STRIP), STRIP)
        total = None
        for r in range(count):
            term = None
            for s, pieces in enumerate((mine[r], other[r])):
                left = jnp.concatenate([piece[:, rows] for piece in pieces], axis=0)
                product = mm(left, cot_ref[r, s], DOT_TN)
                term = product if term is None else term + product
            term = (term * scale).astype(BF).astype(F32)
            total = term if total is None else total + term
        out_ref[rows, :] = total.astype(out_ref.dtype)
        add_products(sums_ref, basis_ref.at[:, rows, :], total)
        return 0

    lax.fori_loop(0, out_ref.shape[0] // STRIP, one, 0)

    @pl.when(step == pl.num_programs(0) - 1)
    def _():
        place_products(tile_ref, sums_ref, basis_ref.shape[0])


def gn_query_products(place, mine, other, cots, basis, scale):
    count = len(mine)
    depth = mine[0][0].shape[1]
    rows, cols = 2 * cots[0].shape[1], cots[0].shape[2]
    stored = basis.shape[0]
    tile = 512
    pieces = [x for group in (*mine, *other) for x in group]
    whole = pl.BlockSpec(cots[0].shape, lambda i, place_ref: (0, 0, 0))
    return pl.pallas_call(
        functools.partial(gn_query_kernel, count, scale),
        grid_spec=pltpu.PrefetchScalarGridSpec(
            num_scalar_prefetch=1,
            grid=(depth // tile,),
            in_specs=[
                pl.BlockSpec((x.shape[0], tile), lambda i, place_ref: (0, i)) for x in pieces
            ]
            + [whole] * (2 * count)
            + [pl.BlockSpec((stored, tile, cols), lambda i, place_ref: (0, i, 0))],
            out_specs=[
                pl.BlockSpec((tile, cols), lambda i, place_ref: (i, 0)),
                pl.BlockSpec((stored, 128), lambda i, place_ref: (0, 0)),
            ],
            scratch_shapes=[
                pltpu.VMEM((rows, cols), BF),
                pltpu.VMEM((count, 2, rows, cols), BF),
                pltpu.VMEM((stored + 1, 8, 128), F32),
            ],
        ),
        out_shape=[
            jax.ShapeDtypeStruct((depth, cols), BF),
            jax.ShapeDtypeStruct((stored, 128), F32),
        ],
        cost_estimate=cost(
            4 * count * rows * depth * cols, 2 * depth * (stored * cols + 2 * count * rows)
        ),
        compiler_params=params(40),
        name="gn_query_products",
    )(place, *pieces, *cots, in_hbm(basis))


def gn_output_kernel(count, scale, last, *refs):
    hts = refs[: 2 * count]
    outs = refs[2 * count : 6 * count]
    if last:
        before_ref, basis_ref, out_ref, tile_ref, head_ref, sums_ref = refs[6 * count :]
    else:
        out_ref, head_ref = refs[6 * count :]
    cols = head_ref.shape[1]
    step = pl.program_id(0)

    @pl.when(step == 0)
    def _():
        for m in range(2 * count):
            block = jnp.concatenate([hts[m][0, :, :cols], hts[m][1, :, :cols]], axis=0)
            head_ref[m] = block.T

    if last:
        clear_products(sums_ref, step == 0)

    def one(n, _):
        columns = pl.ds(pl.multiple_of(n * STRIP, STRIP), STRIP)
        total = before_ref[:, columns] if last else None
        for r in range(count):
            term = None
            for m in (2 * r, 2 * r + 1):
                both = jnp.concatenate([outs[2 * m][:, columns], outs[2 * m + 1][:, columns]], axis=0)
                product = mm(head_ref[m], both)
                term = product if term is None else term + product
            term = (term * scale).astype(BF).astype(F32)
            total = term if total is None else total + term
        out_ref[:, columns] = total.astype(out_ref.dtype)
        if last:
            add_products(sums_ref, basis_ref.at[:, :, columns], total)
        return 0

    lax.fori_loop(0, out_ref.shape[1] // STRIP, one, 0)
    if last:

        @pl.when(step == pl.num_programs(0) - 1)
        def _():
            place_products(tile_ref, sums_ref, basis_ref.shape[0])


def gn_output_sum(hts, halves, outs, scale, before=None, basis=None):
    count = len(hts) // 2
    rows, depth = 2 * outs[0].shape[0], outs[0].shape[1]
    cols = hts[0].shape[2] // 2
    tile = 512
    last = basis is not None
    column = pl.BlockSpec((cols, tile), lambda i: (0, i))
    in_specs = [
        pl.BlockSpec((2, rows // 2, ht.shape[2]), lambda i, n=n: (0, n, 0))
        for ht, n in zip(hts, halves)
    ]
    in_specs += [pl.BlockSpec((rows // 2, tile), lambda i: (0, i))] * (4 * count)
    out_specs = [column]
    out_shape = [jax.ShapeDtypeStruct((cols, depth), BF if last else F32)]
    scratch_shapes = [pltpu.VMEM((2 * count, cols, rows), BF)]
    operands = [*hts, *outs]
    flops, moved = 4 * count * rows * depth * cols, 4 * depth * (cols + count * rows)
    if last:
        stored = basis.shape[0]
        in_specs += [column, pl.BlockSpec((stored, cols, tile), lambda i: (0, 0, i))]
        out_specs.append(pl.BlockSpec((stored, 128), lambda i: (0, 0)))
        out_shape.append(jax.ShapeDtypeStruct((stored, 128), F32))
        scratch_shapes.append(pltpu.VMEM((stored + 1, 8, 128), F32))
        operands += [before, in_hbm(basis)]
        moved += 2 * basis.size + 4 * depth * cols
    return pl.pallas_call(
        functools.partial(gn_output_kernel, count, scale, last),
        grid=(depth // tile,),
        in_specs=in_specs,
        out_specs=out_specs,
        out_shape=out_shape,
        scratch_shapes=scratch_shapes,
        cost_estimate=cost(flops, moved),
        compiler_params=params(32),
        name="gn_output_last" if last else "gn_output_first",
    )(*operands)


GRAM_ROWS = 32


def gram_kernel(basis_ref, tile_ref, total_ref):
    stored, rows, width = basis_ref.shape
    size = stored * GRAM_ROWS
    step = pl.program_id(0)

    @pl.when(step == 0)
    def _():
        total_ref[...] = jnp.zeros_like(total_ref)

    group = min(4 if width < 1024 else 1, rows // GRAM_ROWS)

    def one(n, _):
        total = None
        for m in range(group):
            start = pl.multiple_of((n * group + m) * GRAM_ROWS, GRAM_ROWS)
            block = basis_ref[:, pl.ds(start, GRAM_ROWS), :].reshape(size, width)
            product = mm(block, block, DOT_NT)
            total = product if total is None else total + product
        total_ref[...] += total
        return 0

    lax.fori_loop(0, rows // (group * GRAM_ROWS), one, 0)

    @pl.when(step == pl.num_programs(0) - 1)
    def _():
        row = lax.broadcasted_iota(jnp.int32, (size, size), 0)
        column = lax.broadcasted_iota(jnp.int32, (size, size), 1)
        same = jnp.where(row % GRAM_ROWS == column % GRAM_ROWS, total_ref[...], 0.0)
        sums = jnp.concatenate(
            [
                jnp.sum(same[j * GRAM_ROWS : (j + 1) * GRAM_ROWS], axis=0, keepdims=True)
                for j in range(stored)
            ],
            axis=0,
        )
        member = lax.broadcasted_iota(jnp.int32, (stored, size), 1) // GRAM_ROWS
        lane = lax.broadcasted_iota(jnp.int32, (stored, 128), 1)
        tile = jnp.zeros((stored, 128), F32)
        for k in range(stored):
            one = jnp.sum(jnp.where(member == k, sums, 0.0), axis=1, keepdims=True)
            tile = jnp.where(lane == 8 + k, one, tile)
        tile_ref[...] = tile


def basis_specs(basis_query, steps):
    stored, depth, cols = basis_query.shape
    return [
        pl.BlockSpec((stored, depth // steps, cols), lambda i: (0, i, 0)),
        pl.BlockSpec((stored, cols // steps, depth), lambda i: (0, i, 0)),
    ]


def gram(basis):
    stored, rows, width = basis.shape
    steps = 4
    size = stored * GRAM_ROWS
    return pl.pallas_call(
        gram_kernel,
        grid=(steps,),
        in_specs=[pl.BlockSpec((stored, rows // steps, width), lambda i: (0, i, 0))],
        out_specs=pl.BlockSpec((stored, 128), lambda i: (0, 0)),
        out_shape=jax.ShapeDtypeStruct((stored, 128), F32),
        scratch_shapes=[pltpu.VMEM((size, size), F32)],
        cost_estimate=cost(2 * size * basis.size, 2 * basis.size),
        compiler_params=params(20),
        name="gram",
    )(in_hbm(basis))


def clean_kernel(
    param_count, sums_ref, bq_ref, bo_ref, gq_ref, go_ref, nq_ref, no_ref, tile_ref, scalar_ref
):
    stored = bq_ref.shape[0]

    @pl.when(pl.program_id(0) == 0)
    def _():
        sums = sums_ref[...] / param_count
        first = sums[:, 0:1]
        norm = sums[0:1, 1:2]

        def times_gram(x):
            total = sums[:, 8:9] * x[0:1]
            for k in range(1, stored):
                total = total + sums[:, 8 + k : 9 + k] * x[k : k + 1]
            return total

        coeffs = first + (first - times_gram(first))
        change = jnp.sum(coeffs * (times_gram(coeffs) - 2.0 * first), axis=0, keepdims=True)
        beta = jnp.sqrt(jnp.maximum(norm + change, 0.0) + BETA_EPS)
        lane = lax.broadcasted_iota(jnp.int32, (1, 128), 1)
        tile = jnp.broadcast_to(beta, (1, 128))
        for j in range(stored):
            scalar_ref[j] = jnp.sum(coeffs[j : j + 1])
            tile = jnp.where(lane == j, coeffs[j : j + 1], tile)
        scalar_ref[stored] = jnp.sum(1.0 / beta)
        tile_ref[...] = tile

    inverse = scalar_ref[stored]
    coeffs = [scalar_ref[j] for j in range(stored)]
    for basis_ref, g_ref, next_ref in ((bq_ref, gq_ref, nq_ref), (bo_ref, go_ref, no_ref)):
        rows, width = g_ref.shape
        lanes = min(512, width)
        strips = width // lanes

        def one(n, _, basis_ref=basis_ref, g_ref=g_ref, next_ref=next_ref, strips=strips):
            row = pl.ds(pl.multiple_of((n // strips) * 16, 16), 16)
            column = pl.ds(pl.multiple_of((n % strips) * lanes, lanes), lanes)
            total = g_ref[row, column].astype(F32)
            for j in range(stored):
                total = total - coeffs[j] * basis_ref[j, row, column].astype(F32)
            next_ref[row, column] = (total * inverse).astype(BF)
            return 0

        lax.fori_loop(0, rows // 16 * strips, one, 0, unroll=4)


def clean(sums, basis_query, basis_output, gn_query, gn_output, param_count):
    stored, depth, cols = basis_query.shape
    steps = 8
    query_spec = pl.BlockSpec((depth // steps, cols), lambda i: (i, 0))
    output_spec = pl.BlockSpec((cols // steps, depth), lambda i: (i, 0))
    return pl.pallas_call(
        functools.partial(clean_kernel, param_count),
        grid=(steps,),
        in_specs=[pl.BlockSpec((stored, 128), lambda i: (0, 0))]
        + basis_specs(basis_query, steps)
        + [query_spec, output_spec],
        out_specs=[query_spec, output_spec, pl.BlockSpec((1, 128), lambda i: (0, 0))],
        out_shape=[
            jax.ShapeDtypeStruct((depth, cols), BF),
            jax.ShapeDtypeStruct((cols, depth), BF),
            jax.ShapeDtypeStruct((1, 128), F32),
        ],
        scratch_shapes=[pltpu.SMEM((2 * stored,), F32)],
        cost_estimate=cost(40 * depth * cols, 52 * depth * cols),
        compiler_params=params(40),
        name="clean",
    )(sums, in_hbm(basis_query), in_hbm(basis_output), gn_query, gn_output)


def right_kernel(scale, dir_ref, weight_ref, out_ref):
    out_ref[0] = (dir_ref[0].astype(F32) * scale).astype(BF)
    out_ref[1] = weight_ref[...]


def right_operand(basis, weight, scale):
    last = basis.shape[0] - 1
    cols, depth = weight.shape
    steps = 4
    tile = cols // steps
    out = pl.pallas_call(
        functools.partial(right_kernel, scale),
        grid=(steps,),
        in_specs=[
            pl.BlockSpec((1, tile, depth), lambda i: (last, i, 0)),
            pl.BlockSpec((tile, depth), lambda i: (i, 0)),
        ],
        out_specs=pl.BlockSpec((2, tile, depth), lambda i: (0, i, 0)),
        out_shape=jax.ShapeDtypeStruct((2, cols, depth), BF),
        cost_estimate=cost(cols * depth, 8 * cols * depth),
        compiler_params=params(12),
        name="right_operand",
    )(in_hbm(basis), weight)
    return out.reshape(2 * cols, depth)


def exchange(x, axis, r):
    return lax.ppermute(x, axis, [(i, i ^ r) for i in range(lax.axis_size(axis))])


def line_pairs(links):
    return [(2 * a + core, 2 * b + core) for a, b in links for core in range(2)]


def line_move(x, links):
    return lax.ppermute(x, "tensor", line_pairs(links))


def line_links():
    chips = lax.axis_size("tensor") // 2
    return [((s, s + 1), (chips - 1 - s, chips - 2 - s)) for s in range(chips // 2 - 1)]


def line_sum(x, taken):
    chips = lax.axis_size("tensor") // 2

    def add(a, b):
        return (a.astype(F32) + b.astype(F32)).astype(BF)

    inward = line_links()
    for pair in inward:
        x = add(x, line_move(x, pair))
    middle = ((chips // 2 - 1, chips // 2), (chips // 2, chips // 2 - 1))
    x = add(x, line_move(x, middle))
    for s, ((low, low_next), (high, high_next)) in reversed(list(enumerate(inward))):
        back = line_move(x, ((low_next, low), (high_next, high)))
        x = jnp.where(taken[s], back, x)
    return x


def sum_everywhere(x):
    steps = [("tensor", 1)]
    for axis, start in (("dp", 1), ("tensor", 2)):
        r = start
        while r < lax.axis_size(axis):
            steps.append((axis, r))
            r *= 2
    for axis, r in steps:
        x = x + exchange(x, axis, r)
    return x


def step(tokens, segments, norm_gain, q_weight, kv_weight, o_weight, basis_query, basis_output):
    groups = lax.axis_size("dp")
    seqs, length, width = tokens.shape
    cols = q_weight.shape[1]
    heads = cols // HD
    stored = basis_query.shape[0]
    qwidth = cols * lax.axis_size("tensor")
    query_scale = width ** (-0.5)
    output_scale = qwidth ** (-0.5)
    gn_scale = qwidth / (seqs * length * groups)
    param_count = 2.0 * width * qwidth
    rows = seqs // 2 * length
    assert seqs == 2
    dp = lax.axis_index("dp")
    tensor = lax.axis_index("tensor")
    kv_head = lax.div(tensor * heads, QH // KVH)
    chip = tensor >> 1
    far = rows * 5 // 8 // ROWS
    low = far * (chip & 1)
    place = jnp.stack([tensor & 1, dp, kv_head, low, rows * 3 // 8 // ROWS, far - low])
    place = place.astype(jnp.int32)
    taken = [(chip == low) | (chip == high) for (low, _), (high, _) in line_links()]
    place, taken = lax.optimization_barrier((place, taken))
    table = jnp.asarray(rope_tables(length))

    flat_tokens, gain = tokens.reshape(seqs * length, width), norm_gain[None, :]
    sizes = (rows * 3 // 8, rows // 4, rows * 3 // 8)
    normed = []
    for n, size in enumerate(sizes):
        normed.append(
            norm_blocks(place, flat_tokens, gain, size, 3 + n, groups, groups if n < 2 else 1)
        )
    mine = [[x[0] for x in normed]]
    for r in range(1, groups):
        near = exchange(normed[0][r], "dp", r)
        middle = exchange(normed[1][r], "dp", r)
        mine.append([near, middle, exchange(near, "tensor", 2)])
    other = [[exchange(x, "tensor", 1) for x in group] for group in mine]
    query_parts, tangent_parts = [], []
    for r in range(groups):
        query_part, tangent_part = project(
            place, mine[r], other[r], q_weight, basis_query, kv_weight, query_scale
        )
        query_parts.append(query_part)
        tangent_parts.append(tangent_part)
    bits = [1 << n for n in range(groups.bit_length() - 1)]
    query_parts = halving(query_parts, bits)
    tangent_parts = halving(tangent_parts, bits[::-1])
    ht, ht0, ht1, probs, keys, values = attend(
        place, query_parts, tangent_parts, segments, table, heads
    )

    grams = []
    for basis in (basis_query, basis_output):
        grams.append(gram(basis))

    right = right_operand(basis_output, o_weight, output_scale)
    hts = [[(ht0, 0), (ht1, 0)], [(exchange(x, "dp", 1), 0) for x in (ht0, ht1)]]
    for r in range(2, groups):
        moved = exchange(ht, "dp", r)
        hts.append([(moved, 0), (moved, 1)])
    outs = [[None, None] for _ in range(groups)]
    cots = [[None, None] for _ in range(groups)]
    half = length // 2
    for r, n in chunk_order(groups):
        ht_now, part = hts[r][n]
        ht_rows = ht_now[:, part * half : (part + 1) * half]
        terms = mm(ht_rows.reshape(2 * half, 2 * cols), right).astype(BF)
        given = exchange(terms[half:], "tensor", 1)
        kept = (terms[:half].astype(F32) + given.astype(F32)).astype(BF)
        kept = line_sum(kept, taken)
        swapped = exchange(kept, "tensor", 1)
        outs[r][n] = (kept, swapped)
        out = jnp.concatenate([kept, swapped], axis=0)
        cots[r][n] = mm(out, o_weight, DOT_NT).astype(BF).reshape(2, half, cols)
    cot_moved = [exchange(jnp.stack(cots[1]), "dp", 1)]
    cot_halves = [[exchange(cots[r][n], "dp", r) for r in range(2, groups)] for n in range(2)]

    back = []
    for n in range(2):
        cot_query = attend_transpose(
            [cots[0][n], *cot_halves[n], *cot_moved], probs, keys, values, table, heads, n
        )
        back.append([cot_query] + [exchange(cot_query, "dp", r) for r in range(1, groups)])

    def output_sum(blocks, **rest):
        pieces = [hts[r][n] for r in blocks for n in range(2)]
        return gn_output_sum(
            [x for x, _ in pieces],
            [n for _, n in pieces],
            [x for r in blocks for n in range(2) for x in outs[r][n]],
            gn_scale * output_scale,
            **rest,
        )

    (before,) = output_sum(range(1, groups - 1))
    gn_output, output_tile = output_sum([groups - 1, 0], before=before, basis=basis_output)
    gn_query, query_tile = gn_query_products(
        place,
        mine,
        other,
        [back[n][r] for r in range(groups) for n in range(2)],
        basis_query,
        gn_scale * query_scale,
    )
    sums = sum_everywhere(query_tile + (output_tile + (grams[0] + grams[1])))
    next_query, next_output, tile = clean(
        sums, basis_query, basis_output, gn_query, gn_output, param_count
    )
    return next_query, next_output, tile[0, : stored + 1]


def halving(parts, bits):
    parts = dict(enumerate(parts))
    own = [parts[0]]
    for bit in bits:
        for r in sorted(parts, reverse=True):
            if r & bit:
                moved = exchange(parts.pop(r), "dp", bit)
                if r == bit:
                    own.append(moved)
                else:
                    kept = parts[r ^ bit]
                    parts[r ^ bit] = (kept.astype(F32) + moved.astype(F32)).astype(BF)
    return own


def chunk_order(groups):
    return [(0, 0)] + [(r, n) for r in range(1, groups) for n in range(2)] + [(0, 1)]


def solution(mesh):
    return jax.shard_map(
        step,
        mesh=mesh,
        in_specs=(
            P("dp", None, None),
            P("dp", None),
            P(),
            P("dp", "tensor"),
            P(None, "dp", None),
            P("tensor", "dp"),
            P(None, "dp", "tensor"),
            P(None, "tensor", "dp"),
        ),
        out_specs=(P("dp", "tensor"), P("tensor", "dp"), P()),
        check_vma=False,
    )
```

```python
import functools
import math

import jax
import jax.numpy as jnp
import numpy as np
from jax import lax
from jax.experimental import pallas as pl
from jax.experimental.pallas import tpu as pltpu
from jax.sharding import PartitionSpec as P


HD = 128
QH = 32
KVH = 4
ROPE_BASE = 500000.0
NORM_EPS = 1e-05
BETA_EPS = 1e-06

BF = jnp.bfloat16
F32 = jnp.float32


DOT_NN = (((1,), (0,)), ((), ()))
DOT_NT = (((1,), (1,)), ((), ()))
DOT_TN = (((0,), (0,)), ((), ()))


def mm(a, b, dims=DOT_NN):
    return lax.dot_general(a, b, dims, preferred_element_type=F32)


def split2(x):
    high = x.astype(BF)
    return high, (x - high.astype(F32)).astype(BF)


def mm3(a, b, dims=DOT_NN):
    a_high, a_low = a
    b_high, b_low = b
    return mm(a_high, b_high, dims) + (mm(a_high, b_low, dims) + mm(a_low, b_high, dims))


def cost(flops, bytes_accessed):
    return pl.CostEstimate(flops=int(flops), bytes_accessed=int(bytes_accessed), transcendentals=0)


def params(limit_mib):
    return pltpu.CompilerParams(vmem_limit_bytes=limit_mib << 20)


def in_hbm(x):
    return pltpu.with_memory_space_constraint(x, pltpu.HBM)


def rope_tables(length):
    half = HD // 2
    frequency = np.exp(
        np.arange(half, dtype=np.float32) * np.float32(-2.0 * math.log(ROPE_BASE) / HD)
    ).astype(np.float32)
    angles = np.arange(length, dtype=np.float32)[:, None] * frequency[None, :]
    cosine = np.cos(angles).astype(np.float32)
    sine = np.sin(angles).astype(np.float32)
    return np.concatenate([cosine, sine], axis=1)


def table_pair(table):
    half = table.shape[1] // 2
    cosine, sine = table[:, :half], table[:, half:]
    return jnp.concatenate([cosine, cosine], axis=1), jnp.concatenate([-sine, sine], axis=1)


def swap_halves(x):
    half = x.shape[-1] // 2
    return jnp.concatenate([x[:, half:], x[:, :half]], axis=-1)


ROWS = 32


def norm_kernel(groups, place_ref, x_ref, gain_ref, *out_refs):
    block = x_ref.shape[1] // groups
    mine = place_ref[1]
    total = None
    for e in range(groups):
        part = x_ref[:, e * block : (e + 1) * block].astype(F32)
        part = jnp.sum(part * part, axis=1, keepdims=True)
        total = part if total is None else total + part
    inv_rms = lax.rsqrt(total / x_ref.shape[1] + NORM_EPS)
    for r, out_ref in enumerate(out_refs):
        offset = pl.multiple_of((mine ^ r) * block, block)
        part = x_ref[:, pl.ds(offset, block)].astype(F32)
        gain = gain_ref[:, pl.ds(offset, block)]
        out_ref[...] = (part * inv_rms * gain).astype(BF)


def norm_blocks(place, flat_tokens, gain, rows, which, groups, count):
    width = flat_tokens.shape[1]
    block = width // groups
    steps = rows // ROWS
    half = flat_tokens.shape[0] // (2 * ROWS)
    return pl.pallas_call(
        functools.partial(norm_kernel, groups),
        grid_spec=pltpu.PrefetchScalarGridSpec(
            num_scalar_prefetch=1,
            grid=(steps,),
            in_specs=[
                pl.BlockSpec(
                    (ROWS, width),
                    lambda i, place_ref: (place_ref[0] * half + place_ref[which] + i, 0),
                ),
                pl.BlockSpec((1, width), lambda i, place_ref: (0, 0)),
            ],
            out_specs=[pl.BlockSpec((ROWS, block), lambda i, place_ref: (i, 0))] * count,
        ),
        out_shape=[jax.ShapeDtypeStruct((rows, block), BF)] * count,
        cost_estimate=cost(rows * width * 8, rows * width * 4),
        compiler_params=params(24),
        name="norm_blocks",
    )(place, in_hbm(flat_tokens), gain)


def piece_offsets(place_ref, rows):
    low, high = place_ref[3] * ROWS, place_ref[5] * ROWS
    return (
        (pl.multiple_of(low, ROWS), rows * 3 // 8),
        (rows * 3 // 8, rows // 4),
        (pl.multiple_of(high, ROWS), rows * 3 // 8),
    )


def project_kernel(scale, place_ref, *refs):
    mine, other = refs[:3], refs[3:6]
    q_ref, t_ref, k_ref, v_ref = refs[6:10]
    outs = refs[10:]
    tile = q_ref.shape[1]
    step = pl.program_id(0)
    columns = pl.ds(pl.multiple_of(step * tile, tile), tile)
    pieces = piece_offsets(place_ref, outs[0].shape[1])

    def over(columns, triples):
        for (offset, size), mine_ref, other_ref in zip(pieces, mine, other):
            rows = pl.ds(offset, size)
            both = jnp.concatenate([mine_ref[...], other_ref[...]], axis=0)
            for out_ref, weight, factor in triples:
                product = mm(both, weight())
                product = (product if factor is None else product * factor).astype(BF)
                out_ref[0, rows, columns] = product[:size]
                out_ref[1, rows, columns] = product[size:]

    over(
        columns,
        ((outs[0], lambda: q_ref[...], None), (outs[1], lambda: t_ref[0], scale)),
    )

    @pl.when(step == 0)
    def _():
        last = slice(outs[0].shape[2] - HD, outs[0].shape[2])
        over(last, ((outs[0], lambda: k_ref[0], None), (outs[1], lambda: v_ref[0], None)))


def project(place, mine, other, q_weight, basis_query, kv_weight, scale):
    rows, depth = sum(x.shape[0] for x in mine), mine[0].shape[1]
    cols = q_weight.shape[1]
    tile = min(256, cols)
    last = basis_query.shape[0] - 1
    shape = (2, rows, cols + HD)
    return pl.pallas_call(
        functools.partial(project_kernel, scale),
        grid_spec=pltpu.PrefetchScalarGridSpec(
            num_scalar_prefetch=1,
            grid=(cols // tile,),
            in_specs=[
                pl.BlockSpec(x.shape, lambda i, place_ref: (0, 0)) for x in (*mine, *other)
            ]
            + [
                pl.BlockSpec((depth, tile), lambda i, place_ref: (0, i)),
                pl.BlockSpec((1, depth, tile), lambda i, place_ref: (last, 0, i)),
                pl.BlockSpec((1, depth, HD), lambda i, place_ref: (0, 0, place_ref[2])),
                pl.BlockSpec((1, depth, HD), lambda i, place_ref: (1, 0, place_ref[2])),
            ],
            out_specs=[pl.BlockSpec(shape, lambda i, place_ref: (0, 0, 0))] * 2,
        ),
        out_shape=[jax.ShapeDtypeStruct(shape, BF)] * 2,
        cost_estimate=cost(8 * rows * depth * (cols + HD), 4 * depth * (cols + HD + rows)),
        compiler_params=params(24),
        name="project",
    )(place, *mine, *other, q_weight, in_hbm(basis_query), kv_weight, kv_weight)


def attend_kernel(count, heads, place_ref, *refs):
    query_parts = refs[:count]
    tangent_parts = refs[count : 2 * count]
    table_ref, segment_ref = refs[2 * count : 2 * count + 2]
    whole_ref, *half_refs = refs[2 * count + 2 : 2 * count + 5]
    prob_ref, key_ref, value_ref = refs[2 * count + 5 :]
    length = table_ref.shape[0]
    cols = heads * HD
    cosine, sine = table_pair(table_ref[...])

    def summed(parts, start):
        columns = pl.ds(pl.multiple_of(start, HD), HD)
        total = parts[0][0, :, columns].astype(F32)
        for part in parts[1:]:
            total = total + part[0, :, columns].astype(F32)
        return total.astype(BF)

    def turned(x):
        x = x.astype(F32)
        return x * cosine + swap_halves(x) * sine

    keys = turned(summed(query_parts, cols))
    values = summed(tangent_parts, cols)
    key_ref[0] = keys
    value_ref[0] = values
    key_pair = split2(keys)
    row = lax.broadcasted_iota(jnp.int32, (length, length), 0)
    column = lax.broadcasted_iota(jnp.int32, (length, length), 1)
    segment = jnp.where(
        (pl.program_id(0) + place_ref[0]) % 2 == 0, segment_ref[0:1], segment_ref[1:2]
    )
    segment = jnp.broadcast_to(segment.astype(F32), (length, length))
    allowed = jnp.logical_and(row >= column, segment == segment.T)
    half = length // 2

    def one(h, _):
        query = split2(turned(summed(query_parts, h * HD)))
        tangent = split2(turned(summed(tangent_parts, h * HD)))
        scores = jnp.where(allowed, mm3(query, key_pair, DOT_NT) * HD ** (-0.5), -1e30)
        weights = jnp.exp(scores - jnp.max(scores, axis=-1, keepdims=True))
        probs = weights / jnp.sum(weights, axis=-1, keepdims=True)
        moved = mm3(tangent, key_pair, DOT_NT) * HD ** (-0.5)
        weighted = probs * moved
        moved_probs = weighted - probs * jnp.sum(weighted, axis=-1, keepdims=True)
        prob_ref[0, h] = probs
        for source, base in ((probs, 0), (moved_probs, cols)):
            high, low = split2(source)
            result = (mm(high, values) + mm(low, values)).astype(BF)
            columns = pl.ds(pl.multiple_of(base + h * HD, HD), HD)
            whole_ref[0, :, columns] = result
            for n in range(2):
                half_refs[n][0, :, columns] = result[n * half : (n + 1) * half]
        return 0

    lax.fori_loop(0, heads, one, 0, unroll=2)


def attend(place, query_parts, tangent_parts, segments, table, heads):
    seqs, length, width = query_parts[0].shape
    cols = heads * HD
    one = lambda *shape: pl.BlockSpec(
        (1, *shape), lambda s, place_ref: (s,) + (0,) * len(shape)
    )
    table_spec = pl.BlockSpec((length, HD), lambda s, place_ref: (0, 0))
    return pl.pallas_call(
        functools.partial(attend_kernel, len(query_parts), heads),
        grid_spec=pltpu.PrefetchScalarGridSpec(
            num_scalar_prefetch=1,
            grid=(seqs,),
            in_specs=[one(length, width)] * (2 * len(query_parts))
            + [table_spec, pl.BlockSpec((seqs, length), lambda s, place_ref: (0, 0))],
            out_specs=[
                one(length, 2 * cols),
                one(length // 2, 2 * cols),
                one(length // 2, 2 * cols),
                one(heads, length, length),
                one(length, HD),
                one(length, HD),
            ],
        ),
        out_shape=[
            jax.ShapeDtypeStruct((seqs, length, 2 * cols), BF),
            jax.ShapeDtypeStruct((seqs, length // 2, 2 * cols), BF),
            jax.ShapeDtypeStruct((seqs, length // 2, 2 * cols), BF),
            jax.ShapeDtypeStruct((seqs, heads, length, length), F32),
            jax.ShapeDtypeStruct((seqs, length, HD), F32),
            jax.ShapeDtypeStruct((seqs, length, HD), BF),
        ],
        cost_estimate=cost(seqs * heads * length * length * HD * 24, seqs * length * width * 8),
        compiler_params=params(20),
        name="attend",
    )(place, *query_parts, *tangent_parts, table, segments)


def transpose_kernel(count, heads, *refs):
    parts = refs[:count]
    prob_ref, key_ref, value_ref, table_ref, out_ref = refs[count:]
    key_pair = split2(key_ref[0])
    values = value_ref[0]
    cosine, sine = table_pair(table_ref[...])

    def one(h, _):
        columns = pl.ds(pl.multiple_of(h * HD, HD), HD)
        total = parts[0][0, :, columns].astype(F32)
        for part in parts[1:]:
            part = part.at[0] if len(part.shape) == 4 else part
            total = total + part[0, :, columns].astype(F32)
        high, low = split2(total)
        probs = prob_ref[0, h]
        weighted = probs * (mm(high, values, DOT_NT) + mm(low, values, DOT_NT))
        moved = weighted - probs * jnp.sum(weighted, axis=-1, keepdims=True)
        back = mm3(split2(moved), key_pair) * HD ** (-0.5)
        out_ref[0, :, columns] = (back * cosine - swap_halves(back) * sine).astype(BF)
        return 0

    lax.fori_loop(0, heads, one, 0, unroll=2)


def attend_transpose(parts, probs, keys, values, table, heads, which):
    seqs, rows, cols = parts[0].shape
    length = keys.shape[1]
    one = lambda *shape: pl.BlockSpec((1, *shape), lambda s: (s,) + (0,) * len(shape))
    table_spec = pl.BlockSpec((rows, HD), lambda s: (which, 0))
    return pl.pallas_call(
        functools.partial(transpose_kernel, len(parts), heads),
        grid=(seqs,),
        in_specs=[
            one(rows, cols)
            if part.ndim == 3
            else pl.BlockSpec((1, 1, rows, cols), lambda s: (which, s, 0, 0))
            for part in parts
        ]
        + [
            pl.BlockSpec((1, heads, rows, length), lambda s: (s, 0, which, 0)),
            one(length, HD),
            one(length, HD),
            table_spec,
        ],
        out_specs=one(rows, cols),
        out_shape=jax.ShapeDtypeStruct((seqs, rows, cols), BF),
        cost_estimate=cost(seqs * heads * rows * length * HD * 10, seqs * rows * cols * 16),
        compiler_params=params(16),
        name="attend_transpose",
    )(*parts, probs, keys, values, table)


def fold(x):
    rows, width = x.shape
    x = jnp.sum(x.reshape(rows // 8, 8, width), axis=0)
    total = x[:, :128]
    for start in range(128, width, 128):
        total = total + x[:, start : start + 128]
    return total


STRIP = 256


def clear_products(sums_ref, first):
    @pl.when(first)
    def _():
        sums_ref[...] = jnp.zeros_like(sums_ref)


def add_products(sums_ref, basis_ref, g):
    stored = basis_ref.shape[0]
    for j in range(stored):
        sums_ref[j] += fold(basis_ref[j].astype(F32) * g)
    sums_ref[stored] += fold(g * g)


def place_products(tile_ref, sums_ref, stored):
    row = lax.broadcasted_iota(jnp.int32, (stored, 128), 0)
    lane = lax.broadcasted_iota(jnp.int32, (stored, 128), 1)
    tile = jnp.zeros((stored, 128), F32)
    for j in range(stored):
        tile = jnp.where((row == j) & (lane == 0), jnp.sum(sums_ref[j], keepdims=True), tile)
    tile = jnp.where((row == 0) & (lane == 1), jnp.sum(sums_ref[stored], keepdims=True), tile)
    tile_ref[...] = tile


def gn_query_kernel(count, scale, place_ref, *refs):
    mine = [refs[3 * r : 3 * r + 3] for r in range(count)]
    other = [refs[3 * (count + r) : 3 * (count + r) + 3] for r in range(count)]
    cots = refs[6 * count : 8 * count]
    basis_ref, out_ref, tile_ref, plain_ref, cot_ref, sums_ref = refs[8 * count :]
    half = cots[0].shape[1]
    step = pl.program_id(0)

    @pl.when(step == 0)
    def _():
        for r in range(count):
            for s in range(2):
                for n in range(2):
                    plain_ref[n * half : (n + 1) * half] = cots[2 * r + n][s]
                start = 0
                for offset, size in piece_offsets(place_ref, 2 * half):
                    cot_ref[r, s, start : start + size] = plain_ref[pl.ds(offset, size), :]
                    start += size

    clear_products(sums_ref, step == 0)

    def one(n, _):
        rows = pl.ds(pl.multiple_of(n * STRIP, STRIP), STRIP)
        total = None
        for r in range(count):
            term = None
            for s, pieces in enumerate((mine[r], other[r])):
                left = jnp.concatenate([piece[:, rows] for piece in pieces], axis=0)
                product = mm(left, cot_ref[r, s], DOT_TN)
                term = product if term is None else term + product
            term = (term * scale).astype(BF).astype(F32)
            total = term if total is None else total + term
        out_ref[rows, :] = total.astype(out_ref.dtype)
        add_products(sums_ref, basis_ref.at[:, rows, :], total)
        return 0

    lax.fori_loop(0, out_ref.shape[0] // STRIP, one, 0)

    @pl.when(step == pl.num_programs(0) - 1)
    def _():
        place_products(tile_ref, sums_ref, basis_ref.shape[0])


def gn_query_products(place, mine, other, cots, basis, scale):
    count = len(mine)
    depth = mine[0][0].shape[1]
    rows, cols = 2 * cots[0].shape[1], cots[0].shape[2]
    stored = basis.shape[0]
    tile = 512
    pieces = [x for group in (*mine, *other) for x in group]
    whole = pl.BlockSpec(cots[0].shape, lambda i, place_ref: (0, 0, 0))
    return pl.pallas_call(
        functools.partial(gn_query_kernel, count, scale),
        grid_spec=pltpu.PrefetchScalarGridSpec(
            num_scalar_prefetch=1,
            grid=(depth // tile,),
            in_specs=[
                pl.BlockSpec((x.shape[0], tile), lambda i, place_ref: (0, i)) for x in pieces
            ]
            + [whole] * (2 * count)
            + [pl.BlockSpec((stored, tile, cols), lambda i, place_ref: (0, i, 0))],
            out_specs=[
                pl.BlockSpec((tile, cols), lambda i, place_ref: (i, 0)),
                pl.BlockSpec((stored, 128), lambda i, place_ref: (0, 0)),
            ],
            scratch_shapes=[
                pltpu.VMEM((rows, cols), BF),
                pltpu.VMEM((count, 2, rows, cols), BF),
                pltpu.VMEM((stored + 1, 8, 128), F32),
            ],
        ),
        out_shape=[
            jax.ShapeDtypeStruct((depth, cols), BF),
            jax.ShapeDtypeStruct((stored, 128), F32),
        ],
        cost_estimate=cost(
            4 * count * rows * depth * cols, 2 * depth * (stored * cols + 2 * count * rows)
        ),
        compiler_params=params(40),
        name="gn_query_products",
    )(place, *pieces, *cots, in_hbm(basis))


def gn_output_kernel(count, scale, *refs):
    hts = refs[: 2 * count]
    outs = refs[2 * count : 6 * count]
    basis_ref, out_ref, tile_ref, head_ref, sums_ref = refs[6 * count :]
    cols = head_ref.shape[1]
    step = pl.program_id(0)

    @pl.when(step == 0)
    def _():
        for m in range(2 * count):
            block = jnp.concatenate([hts[m][0, :, :cols], hts[m][1, :, :cols]], axis=0)
            head_ref[m] = block.T

    clear_products(sums_ref, step == 0)

    def one(n, _):
        columns = pl.ds(pl.multiple_of(n * STRIP, STRIP), STRIP)
        total = None
        for r in range(count):
            term = None
            for m in (2 * r, 2 * r + 1):
                both = jnp.concatenate([outs[2 * m][:, columns], outs[2 * m + 1][:, columns]], axis=0)
                product = mm(head_ref[m], both)
                term = product if term is None else term + product
            term = (term * scale).astype(BF).astype(F32)
            total = term if total is None else total + term
        out_ref[:, columns] = total.astype(out_ref.dtype)
        add_products(sums_ref, basis_ref.at[:, :, columns], total)
        return 0

    lax.fori_loop(0, out_ref.shape[1] // STRIP, one, 0)

    @pl.when(step == pl.num_programs(0) - 1)
    def _():
        place_products(tile_ref, sums_ref, basis_ref.shape[0])


def gn_output_products(hts, halves, outs, basis, scale):
    count = len(hts) // 2
    rows, depth = 2 * outs[0].shape[0], outs[0].shape[1]
    cols = hts[0].shape[2] // 2
    stored = basis.shape[0]
    tile = 512
    return pl.pallas_call(
        functools.partial(gn_output_kernel, count, scale),
        grid=(depth // tile,),
        in_specs=[
            pl.BlockSpec((2, rows // 2, ht.shape[2]), lambda i, n=n: (0, n, 0))
            for ht, n in zip(hts, halves)
        ]
        + [pl.BlockSpec((rows // 2, tile), lambda i: (0, i))] * (4 * count)
        + [pl.BlockSpec((stored, cols, tile), lambda i: (0, 0, i))],
        out_specs=[
            pl.BlockSpec((cols, tile), lambda i: (0, i)),
            pl.BlockSpec((stored, 128), lambda i: (0, 0)),
        ],
        out_shape=[
            jax.ShapeDtypeStruct((cols, depth), BF),
            jax.ShapeDtypeStruct((stored, 128), F32),
        ],
        scratch_shapes=[
            pltpu.VMEM((2 * count, cols, rows), BF),
            pltpu.VMEM((stored + 1, 8, 128), F32),
        ],
        cost_estimate=cost(
            4 * count * rows * depth * cols, 2 * depth * (stored * cols + 2 * count * rows)
        ),
        compiler_params=params(36),
        name="gn_output_products",
    )(*hts, *outs, in_hbm(basis))


GRAM_ROWS = 32


def gram_kernel(basis_ref, tile_ref, total_ref):
    stored, rows, width = basis_ref.shape
    size = stored * GRAM_ROWS
    step = pl.program_id(0)

    @pl.when(step == 0)
    def _():
        total_ref[...] = jnp.zeros_like(total_ref)

    group = min(4 if width < 1024 else 1, rows // GRAM_ROWS)

    def one(n, _):
        total = None
        for m in range(group):
            start = pl.multiple_of((n * group + m) * GRAM_ROWS, GRAM_ROWS)
            block = basis_ref[:, pl.ds(start, GRAM_ROWS), :].reshape(size, width)
            product = mm(block, block, DOT_NT)
            total = product if total is None else total + product
        total_ref[...] += total
        return 0

    lax.fori_loop(0, rows // (group * GRAM_ROWS), one, 0)

    @pl.when(step == pl.num_programs(0) - 1)
    def _():
        row = lax.broadcasted_iota(jnp.int32, (size, size), 0)
        column = lax.broadcasted_iota(jnp.int32, (size, size), 1)
        same = jnp.where(row % GRAM_ROWS == column % GRAM_ROWS, total_ref[...], 0.0)
        sums = jnp.concatenate(
            [
                jnp.sum(same[j * GRAM_ROWS : (j + 1) * GRAM_ROWS], axis=0, keepdims=True)
                for j in range(stored)
            ],
            axis=0,
        )
        member = lax.broadcasted_iota(jnp.int32, (stored, size), 1) // GRAM_ROWS
        lane = lax.broadcasted_iota(jnp.int32, (stored, 128), 1)
        tile = jnp.zeros((stored, 128), F32)
        for k in range(stored):
            one = jnp.sum(jnp.where(member == k, sums, 0.0), axis=1, keepdims=True)
            tile = jnp.where(lane == 8 + k, one, tile)
        tile_ref[...] = tile


def basis_specs(basis_query, steps):
    stored, depth, cols = basis_query.shape
    return [
        pl.BlockSpec((stored, depth // steps, cols), lambda i: (0, i, 0)),
        pl.BlockSpec((stored, cols // steps, depth), lambda i: (0, i, 0)),
    ]


def gram(basis):
    stored, rows, width = basis.shape
    steps = 4
    size = stored * GRAM_ROWS
    return pl.pallas_call(
        gram_kernel,
        grid=(steps,),
        in_specs=[pl.BlockSpec((stored, rows // steps, width), lambda i: (0, i, 0))],
        out_specs=pl.BlockSpec((stored, 128), lambda i: (0, 0)),
        out_shape=jax.ShapeDtypeStruct((stored, 128), F32),
        scratch_shapes=[pltpu.VMEM((size, size), F32)],
        cost_estimate=cost(2 * size * basis.size, 2 * basis.size),
        compiler_params=params(20),
        name="gram",
    )(in_hbm(basis))


def clean_kernel(
    param_count, sums_ref, bq_ref, bo_ref, gq_ref, go_ref, nq_ref, no_ref, tile_ref, scalar_ref
):
    stored = bq_ref.shape[0]

    @pl.when(pl.program_id(0) == 0)
    def _():
        sums = sums_ref[...] / param_count
        first = sums[:, 0:1]
        norm = sums[0:1, 1:2]

        def times_gram(x):
            total = sums[:, 8:9] * x[0:1]
            for k in range(1, stored):
                total = total + sums[:, 8 + k : 9 + k] * x[k : k + 1]
            return total

        coeffs = first + (first - times_gram(first))
        change = jnp.sum(coeffs * (times_gram(coeffs) - 2.0 * first), axis=0, keepdims=True)
        beta = jnp.sqrt(jnp.maximum(norm + change, 0.0) + BETA_EPS)
        lane = lax.broadcasted_iota(jnp.int32, (1, 128), 1)
        tile = jnp.broadcast_to(beta, (1, 128))
        for j in range(stored):
            scalar_ref[j] = jnp.sum(coeffs[j : j + 1])
            tile = jnp.where(lane == j, coeffs[j : j + 1], tile)
        scalar_ref[stored] = jnp.sum(1.0 / beta)
        tile_ref[...] = tile

    inverse = scalar_ref[stored]
    coeffs = [scalar_ref[j] for j in range(stored)]
    for basis_ref, g_ref, next_ref in ((bq_ref, gq_ref, nq_ref), (bo_ref, go_ref, no_ref)):
        rows, width = g_ref.shape
        lanes = min(512, width)
        strips = width // lanes

        def one(n, _, basis_ref=basis_ref, g_ref=g_ref, next_ref=next_ref, strips=strips):
            row = pl.ds(pl.multiple_of((n // strips) * 16, 16), 16)
            column = pl.ds(pl.multiple_of((n % strips) * lanes, lanes), lanes)
            total = g_ref[row, column].astype(F32)
            for j in range(stored):
                total = total - coeffs[j] * basis_ref[j, row, column].astype(F32)
            next_ref[row, column] = (total * inverse).astype(BF)
            return 0

        lax.fori_loop(0, rows // 16 * strips, one, 0, unroll=4)


def clean(sums, basis_query, basis_output, gn_query, gn_output, param_count):
    stored, depth, cols = basis_query.shape
    steps = 8
    query_spec = pl.BlockSpec((depth // steps, cols), lambda i: (i, 0))
    output_spec = pl.BlockSpec((cols // steps, depth), lambda i: (i, 0))
    return pl.pallas_call(
        functools.partial(clean_kernel, param_count),
        grid=(steps,),
        in_specs=[pl.BlockSpec((stored, 128), lambda i: (0, 0))]
        + basis_specs(basis_query, steps)
        + [query_spec, output_spec],
        out_specs=[query_spec, output_spec, pl.BlockSpec((1, 128), lambda i: (0, 0))],
        out_shape=[
            jax.ShapeDtypeStruct((depth, cols), BF),
            jax.ShapeDtypeStruct((cols, depth), BF),
            jax.ShapeDtypeStruct((1, 128), F32),
        ],
        scratch_shapes=[pltpu.SMEM((2 * stored,), F32)],
        cost_estimate=cost(40 * depth * cols, 52 * depth * cols),
        compiler_params=params(40),
        name="clean",
    )(sums, in_hbm(basis_query), in_hbm(basis_output), gn_query, gn_output)


def right_kernel(scale, dir_ref, weight_ref, out_ref):
    out_ref[0] = (dir_ref[0].astype(F32) * scale).astype(BF)
    out_ref[1] = weight_ref[...]


def right_operand(basis, weight, scale):
    last = basis.shape[0] - 1
    cols, depth = weight.shape
    steps = 4
    tile = cols // steps
    out = pl.pallas_call(
        functools.partial(right_kernel, scale),
        grid=(steps,),
        in_specs=[
            pl.BlockSpec((1, tile, depth), lambda i: (last, i, 0)),
            pl.BlockSpec((tile, depth), lambda i: (i, 0)),
        ],
        out_specs=pl.BlockSpec((2, tile, depth), lambda i: (0, i, 0)),
        out_shape=jax.ShapeDtypeStruct((2, cols, depth), BF),
        cost_estimate=cost(cols * depth, 8 * cols * depth),
        compiler_params=params(12),
        name="right_operand",
    )(in_hbm(basis), weight)
    return out.reshape(2 * cols, depth)


def exchange(x, axis, r):
    return lax.ppermute(x, axis, [(i, i ^ r) for i in range(lax.axis_size(axis))])


def line_pairs(links):
    return [(2 * a + core, 2 * b + core) for a, b in links for core in range(2)]


def line_move(x, links):
    return lax.ppermute(x, "tensor", line_pairs(links))


def line_links():
    chips = lax.axis_size("tensor") // 2
    return [((s, s + 1), (chips - 1 - s, chips - 2 - s)) for s in range(chips // 2 - 1)]


def line_sum(x, taken):
    chips = lax.axis_size("tensor") // 2

    def add(a, b):
        return (a.astype(F32) + b.astype(F32)).astype(BF)

    inward = line_links()
    for pair in inward:
        moved = line_move(x, pair)
        x = add(x, moved)
    middle = ((chips // 2 - 1, chips // 2), (chips // 2, chips // 2 - 1))
    moved = line_move(x, middle)
    x = add(x, moved)
    for s, ((low, low_next), (high, high_next)) in reversed(list(enumerate(inward))):
        back = line_move(x, ((low_next, low), (high_next, high)))
        x = jnp.where(taken[s], back, x)
    return x


def sum_everywhere(x):
    steps = [("tensor", 1)]
    for axis, start in (("dp", 1), ("tensor", 2)):
        r = start
        while r < lax.axis_size(axis):
            steps.append((axis, r))
            r *= 2
    for axis, r in steps:
        x = x + exchange(x, axis, r)
    return x


def step(tokens, segments, norm_gain, q_weight, kv_weight, o_weight, basis_query, basis_output):
    groups = lax.axis_size("dp")
    seqs, length, width = tokens.shape
    cols = q_weight.shape[1]
    heads = cols // HD
    stored = basis_query.shape[0]
    qwidth = cols * lax.axis_size("tensor")
    query_scale = width ** (-0.5)
    output_scale = qwidth ** (-0.5)
    gn_scale = qwidth / (seqs * length * groups)
    param_count = 2.0 * width * qwidth
    rows = seqs // 2 * length
    assert seqs == 2
    dp = lax.axis_index("dp")
    tensor = lax.axis_index("tensor")
    kv_head = lax.div(tensor * heads, QH // KVH)
    chip = tensor >> 1
    far = rows * 5 // 8 // ROWS
    low = far * (chip & 1)
    place = jnp.stack([tensor & 1, dp, kv_head, low, rows * 3 // 8 // ROWS, far - low])
    place = place.astype(jnp.int32)
    taken = [(chip == low) | (chip == high) for (low, _), (high, _) in line_links()]
    place, taken = lax.optimization_barrier((place, taken))
    table = jnp.asarray(rope_tables(length))

    flat_tokens, gain = tokens.reshape(seqs * length, width), norm_gain[None, :]
    sizes = (rows * 3 // 8, rows // 4, rows * 3 // 8)
    normed = []
    for n, size in enumerate(sizes):
        normed.append(
            norm_blocks(place, flat_tokens, gain, size, 3 + n, groups, groups if n < 2 else 1)
        )
    mine = [[x[0] for x in normed]]
    for r in range(1, groups):
        near = exchange(normed[0][r], "dp", r)
        middle = exchange(normed[1][r], "dp", r)
        mine.append([near, middle, exchange(near, "tensor", 2)])
    other = [[exchange(x, "tensor", 1) for x in group] for group in mine]
    query_parts, tangent_parts = [], []
    for r in range(groups):
        query_part, tangent_part = project(
            place, mine[r], other[r], q_weight, basis_query, kv_weight, query_scale
        )
        query_parts.append(query_part)
        tangent_parts.append(tangent_part)
    bits = [1 << n for n in range(groups.bit_length() - 1)]
    query_parts = halving(query_parts, bits)
    tangent_parts = halving(tangent_parts, bits[::-1])
    ht, ht0, ht1, probs, keys, values = attend(
        place, query_parts, tangent_parts, segments, table, heads
    )

    grams = []
    for basis in (basis_query, basis_output):
        grams.append(gram(basis))

    right = right_operand(basis_output, o_weight, output_scale)
    hts = [[(ht0, 0), (ht1, 0)], [(exchange(x, "dp", 1), 0) for x in (ht0, ht1)]]
    for r in range(2, groups):
        moved = exchange(ht, "dp", r)
        hts.append([(moved, 0), (moved, 1)])
    outs = [[None, None] for _ in range(groups)]
    cots = [[None, None] for _ in range(groups)]
    half = length // 2
    for r, n in chunk_order(groups):
        ht_now, part = hts[r][n]
        ht_rows = ht_now[:, part * half : (part + 1) * half]
        terms = mm(ht_rows.reshape(2 * half, 2 * cols), right).astype(BF)
        given = exchange(terms[half:], "tensor", 1)
        kept = (terms[:half].astype(F32) + given.astype(F32)).astype(BF)
        kept = line_sum(kept, taken)
        swapped = exchange(kept, "tensor", 1)
        outs[r][n] = (kept, swapped)
        out = jnp.concatenate([kept, swapped], axis=0)
        cots[r][n] = mm(out, o_weight, DOT_NT).astype(BF).reshape(2, half, cols)
    cot_moved = [exchange(jnp.stack(cots[1]), "dp", 1)]
    cot_halves = [[exchange(cots[r][n], "dp", r) for r in range(2, groups)] for n in range(2)]

    back = []
    for n in range(2):
        cot_query = attend_transpose(
            [cots[0][n], *cot_halves[n], *cot_moved], probs, keys, values, table, heads, n
        )
        back.append([cot_query] + [exchange(cot_query, "dp", r) for r in range(1, groups)])

    pieces = [(hts[r][n], outs[r][n]) for r in range(groups) for n in range(2)]
    gn_output, output_tile = gn_output_products(
        [ht for (ht, _), _ in pieces],
        [n for (_, n), _ in pieces],
        [x for _, both in pieces for x in both],
        basis_output,
        gn_scale * output_scale,
    )
    gn_query, query_tile = gn_query_products(
        place,
        mine,
        other,
        [back[n][r] for r in range(groups) for n in range(2)],
        basis_query,
        gn_scale * query_scale,
    )
    sums = sum_everywhere(query_tile + (output_tile + (grams[0] + grams[1])))
    next_query, next_output, tile = clean(
        sums, basis_query, basis_output, gn_query, gn_output, param_count
    )
    return next_query, next_output, tile[0, : stored + 1]


def halving(parts, bits):
    parts = dict(enumerate(parts))
    own = [parts[0]]
    for bit in bits:
        for r in sorted(parts, reverse=True):
            if r & bit:
                moved = exchange(parts.pop(r), "dp", bit)
                if r == bit:
                    own.append(moved)
                else:
                    kept = parts[r ^ bit]
                    parts[r ^ bit] = (kept.astype(F32) + moved.astype(F32)).astype(BF)
    return own


def chunk_order(groups):
    return [(0, 0)] + [(r, n) for r in range(1, groups) for n in range(2)] + [(0, 1)]


def solution(mesh):
    return jax.shard_map(
        step,
        mesh=mesh,
        in_specs=(
            P("dp", None, None),
            P("dp", None),
            P(),
            P("dp", "tensor"),
            P(None, "dp", None),
            P("tensor", "dp"),
            P(None, "dp", "tensor"),
            P(None, "tensor", "dp"),
        ),
        out_specs=(P("dp", "tensor"), P("tensor", "dp"), P()),
        check_vma=False,
    )
```
